512 devices in a mesh: labels: 128 (over y, z, core), heads: 4 (over x).
Axes of the slice: x: 4, y: 4, z: 16, core: 2. Of those that a mesh axis runs over, the one named last changes fastest.
Arguments:
- hidden_in: bfloat16 [65536, 768], P('labels', 'heads'), may hold values from -6 to 6
- w_up: bfloat16 [768, 3072], P(None, 'heads'), may hold values from -0.21875 to 0.21875
- w_down: bfloat16 [3072, 768], P('heads'), may hold values from -0.109375 to 0.109375
- norm_gain: float32 [768], replicated, may hold values from 0.25 to 1.75
- title_length: int32 [4096], P('labels'), may hold values from 1 to 16
- label_leaf: int32 [4096], P('labels'), may hold values from 0 to 1023, as said below
- leaf_parent: int32 [1024], P('labels'), may hold values from 0 to 255
Outputs:
- label_embed: bfloat16 [4096, 768], P('labels')
- leaf_centers: float32 [1024, 768], P('labels', 'heads')
- parent_sums: float32 [256, 768], P('labels', 'heads')
The draws below stay inside these ranges and needn't reach their ends.
Inputs may be any that keep to these rules, and one draw needn't show every extreme that they name: `label_leaf`: leaf l belongs to owner l // 8. The 32 labels of one device (an aligned block of 32 labels) name leaves of any one owner at most 2 times; in every draw one owner is named exactly 2 times by every device.
All inputs are finite; a program needn't handle non-finite values.
Results may differ from the reference program's by a relative error of at most 0.009.
Values may be sent and summed in bfloat16 or wider, within the bound.
A program may use at most 64 MiB of HBM per device.

```python
import math
import jax
import jax.numpy as jnp
from jax import lax

D = 768
FF = 3072
SEQ = 16
LAB_DEV = 32
LEAF_DEV = 8
LABELS = 4096
LEAVES = 1024
PARENTS = 256
CAP = 2
N_HEADS = 4


def draw_label_leaf(key, part):
    owner_total = LABELS // LAB_DEV
    hot_owner = jax.random.randint(jax.random.fold_in(key, 7), (), 0, owner_total)

    def for_device(device):
        device_key = jax.random.fold_in(key, device + 1000)
        slot_ids = jax.random.permutation(jax.random.fold_in(device_key, 1), owner_total * CAP)
        slot_owner = slot_ids // CAP
        ranking_key = jnp.where(slot_owner == hot_owner, owner_total * CAP, 0) + jnp.arange(owner_total * CAP)
        ordering = jnp.argsort(ranking_key)
        remaining = slot_ids[ordering[:LAB_DEV - CAP]]
        picked_slots = jnp.concatenate([hot_owner * CAP + jnp.arange(CAP), remaining])
        picked_slots = picked_slots[jax.random.permutation(jax.random.fold_in(device_key, 2), LAB_DEV)]
        inner_leaf = jax.random.randint(jax.random.fold_in(device_key, 3), (LAB_DEV,), 0, LEAF_DEV)
        return picked_slots // CAP * LEAF_DEV + inner_leaf
    return jax.vmap(for_device)(jnp.arange(owner_total)).reshape(-1).astype(jnp.int32)


def set_ends(result, key, least, high):
    place = [jax.random.randint(jax.random.fold_in(key, axis), (), 0, length) for axis, length in enumerate(result.shape)]
    longest = result.shape.index(max(result.shape))
    neighbour = place[:longest] + [(place[longest] + 1) % result.shape[longest]] + place[longest + 1:]
    return result.at[tuple(place)].set(least).at[tuple(neighbour)].set(high)


def shard_levels(rng, shape, split, smallest, high):
    def one(position, blocks):
        draws = jax.random.uniform(jax.random.fold_in(jax.random.fold_in(rng, 6), position), (blocks,), jnp.float32, smallest / len(split), high / len(split))
        return jnp.repeat(jnp.exp(draws), shape[position] // blocks).reshape((-1,) + (1,) * (len(shape) - position - 1))

    gain = one(*split[0])
    for cut in split[1:]:
        gain = gain * one(*cut)
    return gain


def normal_values(key, extent, spread, limit, split=(), dtype=jnp.bfloat16):
    array = jax.random.normal(key, extent, jnp.float32) * spread
    if len(split) > 0:
        array = shard_levels(key, extent, split, -0.22, 0.18) * array
    return jnp.clip(array, min=-limit, max=limit).astype(dtype)


def setup_inputs(seed: int = 0) -> dict:
    arg_keys = jax.random.split(jax.random.key(seed), 8)
    hidden_in = normal_values(arg_keys[0], (LABELS * SEQ, D), 1.0, 6.0, ((0, 128), (1, 4)))
    w_up = normal_values(arg_keys[1], (D, FF), D ** -0.5, 0.21875, ((1, 4),))
    w_down = normal_values(arg_keys[2], (FF, D), FF ** -0.5, 0.109375, ((0, 4),))
    norm_gain = jnp.clip(1.0 + 0.15 * jax.random.normal(arg_keys[3], (D,), jnp.float32), 0.25, 1.75)
    title_length = set_ends(jax.random.randint(arg_keys[4], (LABELS,), 1, SEQ + 1), jax.random.fold_in(arg_keys[4], 1), 1, SEQ).astype(jnp.int32)
    label_leaf = draw_label_leaf(jax.random.fold_in(arg_keys[7], 71), 0)
    leaf_parent = set_ends(jax.random.randint(arg_keys[6], (LEAVES,), 0, PARENTS), jax.random.fold_in(arg_keys[6], 1), 0, PARENTS - 1).astype(jnp.int32)
    return dict(hidden_in=hidden_in, w_up=w_up, w_down=w_down, norm_gain=norm_gain, title_length=title_length, label_leaf=label_leaf, leaf_parent=leaf_parent)


def encode_block(token_block, length_block, w_up, w_down, norm_gain):
    upward = jnp.dot(token_block, w_up, preferred_element_type=jnp.float32)
    activ = jax.nn.gelu(upward, approximate=False).astype(jnp.bfloat16)
    block_units = FF // N_HEADS
    total = jnp.zeros((token_block.shape[0], D), jnp.float32)
    for head_block in range(N_HEADS):
        piece = jnp.dot(activ[:, head_block * block_units:(head_block + 1) * block_units], w_down[head_block * block_units:(head_block + 1) * block_units], preferred_element_type=jnp.float32).astype(jnp.bfloat16)
        piece = lax.optimization_barrier(piece)
        total = total + piece.astype(jnp.float32)
    mixed = (token_block.astype(jnp.float32) + total).astype(jnp.bfloat16)
    mixed = lax.optimization_barrier(mixed)
    as_float = mixed.astype(jnp.float32)
    mean_value = lax.optimization_barrier(jnp.mean(as_float, axis=1, keepdims=True))
    centred = as_float - mean_value
    variance = lax.optimization_barrier(jnp.mean(centred * centred, axis=1, keepdims=True))
    normed = centred * lax.rsqrt(variance + 1e-05) * norm_gain[None, :]
    grouped = normed.reshape(length_block.shape[0], SEQ, D)
    keep_mask = (jnp.arange(SEQ)[None, :] < length_block[:, None]).astype(jnp.float32)
    pooled = lax.optimization_barrier(jnp.sum(grouped * keep_mask[:, :, None], axis=1)) / length_block.astype(jnp.float32)[:, None]
    scale_inv = lax.rsqrt(lax.optimization_barrier(jnp.mean(pooled * pooled, axis=1, keepdims=True)) + 1e-05)
    return (pooled * scale_inv).astype(jnp.bfloat16)

def reference(hidden_in, w_up, w_down, norm_gain, title_length, label_leaf, leaf_parent):
    block_size = math.gcd(LABELS, 256)
    blocks = LABELS // block_size
    token_blocks = hidden_in.reshape(blocks, block_size * SEQ, D)
    length_blocks = title_length.reshape(blocks, block_size)

    def run_block(operand_pair):
        return encode_block(operand_pair[0], operand_pair[1], w_up, w_down, norm_gain)
    label_embed = lax.map(run_block, (token_blocks, length_blocks)).reshape(LABELS, D)
    leaf_sum = jax.ops.segment_sum(label_embed.astype(jnp.float32), label_leaf, num_segments=LEAVES)
    leaf_centers = leaf_sum * lax.rsqrt(lax.optimization_barrier(jnp.mean(leaf_sum * leaf_sum, axis=1, keepdims=True)) + 1e-05)
    parent_sums = jax.ops.segment_sum(leaf_centers, leaf_parent, num_segments=PARENTS)
    return (label_embed, leaf_centers, parent_sums)
```

```python
import functools

import jax
import jax.numpy as jnp
from jax import lax
from jax.experimental import pallas as pl
from jax.experimental.pallas import tpu as pltpu
from jax.sharding import Mesh
from jax.sharding import PartitionSpec as P

AY, AZ, AC, AX = "labels_0", "labels_1", "labels_2", "heads"
LABELS = (AY, AZ, AC)
NX = 4
SEQ = 16
LAB = 32
LEAF = 8
PAR = 2
PIECES = 4
SHARE = 192
WIDE = 768
PAD = 256
MESH = pl.DeviceIdType.MESH
F32, BF16 = jnp.float32, jnp.bfloat16


def remote(src, dst, send, recv, **where):
    return pltpu.make_async_remote_copy(
        src_ref=src, dst_ref=dst, send_sem=send, recv_sem=recv, device_id=where, device_id_type=MESH
    )


def unpack(rows):
    return jnp.concatenate([rows[:, :SHARE], rows[:, SHARE:]], axis=0)


def kernel(
    ny, nz, nc,
    len_ref, hidden, w_up, w_down, gain_ref, leaf_ref, parent_ref,
    embed_out, centers_out, sums_out,
    hv, hp, upv, downv, from_left, from_right, far, pb, near_left, near_right, rs_left, rs_right,
    hid, table, tables, pick_leaf, pick_parent, blocks, lab, wide, zbuf, zrecv, sbuf, srecv, qrecv,
    pbuf, precv,
    local_sem, ag_send, ag_recv, fwd_send, fwd_recv, d2_send, d2_recv, rs_send, rs_recv,
    t_send, t_recv, s1_send, s1_recv, e_send, e_recv, z1_send, z1_recv,
    s2_send, s2_recv, q_send, q_recv, z2_send, z2_recv,
):
    y, z, c, x = (lax.axis_index(a) for a in (AY, AZ, AC, AX))
    plane = ny * nc
    here = y * nc + c
    right, left, across = lax.rem(x + 1, NX), lax.rem(x + NX - 1, NX), lax.rem(x + 2, NX)

    def mate(k):
        other = lax.rem(here + k, plane)
        return lax.div(other, nc), lax.rem(other, nc)

    fetch = pltpu.make_async_copy(hidden, hv, local_sem.at[0])
    fetch.start()
    loads = []
    for i in range(NX):
        rows = pl.ds(pl.multiple_of(lax.rem(x + i, NX) * SHARE, SHARE), SHARE)
        loads.append(pltpu.make_async_copy(w_up.at[rows], upv.at[i], local_sem.at[1 + i]))
    loads.append(pltpu.make_async_copy(w_down, downv, local_sem.at[1 + NX]))
    for load in loads:
        load.start()

    barrier = pltpu.get_barrier_semaphore()
    for k in range(1, NX):
        pl.semaphore_signal(barrier, 1, device_id={AX: lax.rem(x + k, NX)}, device_id_type=MESH)
    for k in range(1, nz):
        pl.semaphore_signal(barrier, 1, device_id={AZ: lax.rem(z + k, nz)}, device_id_type=MESH)

    @pl.loop(1, plane)
    def _(k):
        yy, cc = mate(k)

        @pl.loop(0, NX)
        def _(i):
            pl.semaphore_signal(barrier, 1, device_id={AY: yy, AC: cc, AX: i}, device_id_type=MESH)

    table[...] = jnp.zeros_like(table)
    table[0:1, 0:LAB] = leaf_ref[...]
    table[1:2, 0:LEAF] = parent_ref[...]
    fetch.wait()
    for p in range(PIECES):
        for j in range(NX):
            first = 128 * j + 32 * p
            hp[p, 16 * j : 16 * j + 16, :] = jnp.concatenate(
                [hv[first : first + 16, :], hv[first + 16 : first + 32, :]], axis=1
            )
    pl.semaphore_wait(barrier, NX - 1 + nz - 1 + (plane - 1) * NX)

    to_right, to_left = {AX: right}, {AX: left}
    ag = []
    for p in range(PIECES):
        ag.append((
            remote(hp.at[p], from_left.at[p], ag_send.at[0, p], ag_recv.at[0, p], **to_right),
            remote(hp.at[p], from_right.at[p], ag_send.at[1, p], ag_recv.at[1, p], **to_left),
        ))
        for copy in ag[p]:
            copy.start()
    low, high = pl.ds(0, 32), pl.ds(32, 32)
    fwd = [
        (
            remote(from_right.at[p, low], far.at[p, low], fwd_send.at[0, p], fwd_recv.at[0, p], **to_left),
            remote(from_left.at[p, high], far.at[p, high], fwd_send.at[1, p], fwd_recv.at[1, p], **to_right),
        )
        for p in range(PIECES)
    ]

    def forward(p):
        ag[p][1].wait_recv()
        fwd[p][0].start()
        ag[p][0].wait_recv()
        fwd[p][1].start()

    @pl.loop(1, plane)
    def _(k):
        yy, cc = mate(k)
        remote(table, tables.at[here], t_send, t_recv, **{AY: yy, AC: cc}).start()

    tables[here] = table[...]

    d2 = [
        (
            remote(pb.at[p, across, 0], near_left.at[p], d2_send.at[0, p], d2_recv.at[0, p], **to_right),
            remote(pb.at[p, across, 1], near_right.at[p], d2_send.at[1, p], d2_recv.at[1, p], **to_left),
        )
        for p in range(PIECES)
    ]
    rs = [
        (
            remote(pb.at[p, right], rs_left.at[p], rs_send.at[0, p], rs_recv.at[0, p], **to_right),
            remote(pb.at[p, left], rs_right.at[p], rs_send.at[1, p], rs_recv.at[1, p], **to_left),
        )
        for p in range(PIECES)
    ]

    def compute(p):
        refs = (hp.at[p], from_right.at[p], far.at[p], from_left.at[p])
        upward = None
        mine = pl.ds(pl.multiple_of(16 * x, 16), 16)
        for i, ref in enumerate(refs):
            term = jnp.dot(unpack(ref[...]), upv[i], preferred_element_type=F32)
            upward = term if upward is None else upward + term
            hid[lax.rem(x + i, NX), 32 * p : 32 * p + 32, :] = unpack(ref[mine, :])
        activ = (0.5 * upward * (1.0 + lax.erf(upward * (0.5**0.5)))).astype(BF16)
        partial = jnp.dot(activ, downv[...], preferred_element_type=F32).astype(BF16)
        for half in range(2):
            for j in range(NX):
                row = 64 * half + 16 * j
                pb[p, j, half] = partial[row : row + 16]

    def finish(p):
        d2[p][0].wait_recv()
        pb[p, right, 0] = (pb[p, right, 0].astype(F32) + near_left[p].astype(F32)).astype(BF16)
        d2[p][1].wait_recv()
        pb[p, left, 1] = (pb[p, left, 1].astype(F32) + near_right[p].astype(F32)).astype(BF16)
        for copy in rs[p]:
            copy.start()

    forward(0)
    for load in loads:
        load.wait()
    for p in range(PIECES):
        if p + 1 < PIECES:
            forward(p + 1)
        for copy in fwd[p]:
            copy.wait_recv()
        compute(p)
        for copy in d2[p]:
            copy.start()
        if p >= 1:
            finish(p - 1)
    finish(PIECES - 1)

    others = tables.at[pl.ds(0, plane - 1)]
    remote(others, others, t_send, t_recv, **to_right).wait_recv()
    column = nz * LEAF
    row = lax.broadcasted_iota(jnp.int32, (column, 1), 0)
    leaf_of_row = ((y * nz + lax.div(row, LEAF)) * nc + c) * LEAF + lax.rem(row, LEAF)
    row2 = lax.broadcasted_iota(jnp.int32, (nz * PAR, 1), 0)
    parent_of_row = ((y * nz + lax.div(row2, PAR)) * nc + c) * PAR + lax.rem(row2, PAR)
    for k in range(plane):
        pick_leaf[:, LAB * k : LAB * (k + 1)] = (leaf_of_row == tables[k, 0:1, 0:LAB]).astype(F32)
        pick_parent[:, LEAF * k : LEAF * (k + 1)] = (parent_of_row == tables[k, 1:2, 0:LEAF]).astype(F32)

    gain = gain_ref[...]
    position = lax.broadcasted_iota(jnp.int32, (SEQ, 1), 0)
    embeds = []
    for p in range(PIECES):
        for copy in rs[p]:
            copy.wait_recv()
        for half in range(2):
            rows = slice(32 * p + 16 * half, 32 * p + 16 * half + 16)
            residual = jnp.concatenate([hid[s, rows, :].astype(F32) for s in range(NX)], axis=1)
            summed = pb[p, x, half].astype(F32) + rs_left[p, half].astype(F32) + rs_right[p, half].astype(F32)
            mixed = (residual + summed).astype(BF16).astype(F32)
            mean = jnp.mean(mixed, axis=1, keepdims=True)
            centred = mixed - mean
            variance = jnp.mean(centred * centred, axis=1, keepdims=True)
            normed = centred * lax.rsqrt(variance + 1e-05) * gain
            length = len_ref[8 * x + 2 * p + half]
            kept = jnp.where(position < length, normed, 0.0)
            pooled = jnp.sum(kept, axis=0, keepdims=True) / length.astype(F32)
            embeds.append(pooled * lax.rsqrt(jnp.mean(pooled * pooled, axis=1, keepdims=True) + 1e-05))
    embed = jnp.concatenate(embeds, axis=0)
    zero = jnp.zeros((8, PAD - SHARE), F32)
    for s in range(NX):
        part = embed[:, SHARE * s : SHARE * (s + 1)]
        blocks[s] = jnp.concatenate([part, zero], axis=1).astype(BF16)

    @pl.loop(0, plane)
    def _(k):
        yy, cc = mate(k)

        @pl.loop(jnp.where(k == 0, 1, 0), NX)
        def _(i):
            to = lax.rem(x + i, NX)
            remote(blocks.at[to], lab.at[here * NX + x], s1_send, s1_recv, **{AY: yy, AC: cc, AX: to}).start()

    for k in range(1, NX):
        remote(blocks, wide.at[x], e_send.at[k], e_recv.at[NX - k], **{AX: lax.rem(x + k, NX)}).start()
    lab[here * NX + x] = blocks[x]
    wide[x] = blocks[...]

    got = lab.at[pl.ds(0, plane * NX - 1)]
    remote(got, got, s1_send, s1_recv, **to_right).wait_recv()
    labels = lab[...].astype(F32).reshape(plane * LAB, PAD).astype(BF16)
    leaf_part = jnp.dot(pick_leaf[...].astype(BF16), labels, preferred_element_type=F32)
    zbuf[...] = leaf_part.reshape(nz, LEAF, PAD).astype(BF16)
    order = sorted(range(1, nz), key=lambda k: -min(k, nz - k))
    for k in order:
        to = lax.rem(z + k, nz)
        remote(zbuf.at[to], zrecv.at[z], z1_send, z1_recv, **{AZ: to}).start()
    zrecv[z] = zbuf[z]

    for k in range(1, NX):
        remote(blocks, wide.at[x], e_send.at[k], e_recv.at[k], **to_right).wait_recv()
    embed_out[...] = jnp.concatenate(
        [
            jnp.concatenate([wide[s, b].astype(F32)[:, :SHARE] for b in range(NX)], axis=1)
            for s in range(NX)
        ],
        axis=0,
    ).astype(BF16)

    got = zrecv.at[pl.ds(0, nz - 1)]
    remote(got, got, z1_send, z1_recv, **to_right).wait_recv()
    leaf_sum = jnp.sum(zrecv[...].astype(F32), axis=0)
    square = jnp.sum(leaf_sum * leaf_sum, axis=1, keepdims=True)
    lane = lax.broadcasted_iota(jnp.int32, (LEAF, PAD), 1)
    sbuf[...] = jnp.where(lane < SHARE, leaf_sum, square)

    @pl.loop(0, plane)
    def _(k):
        yy, cc = mate(k)

        @pl.loop(1, NX)
        def _(i):
            to = {AY: yy, AC: cc, AX: lax.rem(x + i, NX)}
            remote(sbuf.at[:, pl.ds(128, 128)], qrecv.at[x, here], q_send, q_recv, **to).start()

        @pl.when(k > 0)
        def _():
            remote(sbuf, srecv.at[here], s2_send, s2_recv, **{AY: yy, AC: cc}).start()

    srecv[here] = sbuf[...]
    qrecv[x] = jnp.zeros_like(qrecv[x])
    got = srecv.at[pl.ds(0, plane - 1)]
    remote(got, got, s2_send, s2_recv, **to_right).wait_recv()
    got = qrecv.at[pl.ds(0, NX - 1)]
    remote(got, got, q_send, q_recv, **to_right).wait_recv()
    sums = srecv[...]
    total = sums[:, :, PAD - 1 :] + jnp.sum(qrecv[...], axis=0)[:, :, 127:]
    centers = sums * lax.rsqrt(total / WIDE + 1e-05)
    sbuf_mine = srecv[here]
    total_mine = sbuf_mine[:, PAD - 1 :]
    for s in range(NX):
        total_mine = total_mine + qrecv[s, here][:, 127:]
    centers_out[...] = (sbuf_mine * lax.rsqrt(total_mine / WIDE + 1e-05))[:, :SHARE]
    parent_part = jnp.dot(
        pick_parent[...],
        centers.reshape(plane * LEAF, PAD),
        preferred_element_type=F32,
        precision=lax.Precision.HIGHEST,
    )
    for k in range(nz):
        pbuf[k] = parent_part[PAR * k : PAR * (k + 1)]
    for k in order:
        to = lax.rem(z + k, nz)
        remote(pbuf.at[to], precv.at[z], z2_send, z2_recv, **{AZ: to}).start()
    precv[z] = pbuf[z]
    got = precv.at[pl.ds(0, nz - 1)]
    remote(got, got, z2_send, z2_recv, **to_right).wait_recv()
    sums_out[...] = jnp.sum(precv[...], axis=0)[:, :SHARE]

    for p in range(PIECES):
        for copy in (*ag[p], *fwd[p], *d2[p], *rs[p]):
            copy.wait_send()
    remote(others, others, t_send, t_recv, **to_right).wait_send()
    got = lab.at[pl.ds(0, plane * NX - 1)]
    remote(got, got, s1_send, s1_recv, **to_right).wait_send()
    for k in range(1, NX):
        remote(blocks, wide.at[x], e_send.at[k], e_recv.at[k], **to_right).wait_send()
    got = zrecv.at[pl.ds(0, nz - 1)]
    remote(got, got, z1_send, z1_recv, **to_right).wait_send()
    got = srecv.at[pl.ds(0, plane - 1)]
    remote(got, got, s2_send, s2_recv, **to_right).wait_send()
    got = qrecv.at[pl.ds(0, NX - 1)]
    remote(got, got, q_send, q_recv, **to_right).wait_send()
    got = precv.at[pl.ds(0, nz - 1)]
    remote(got, got, z2_send, z2_recv, **to_right).wait_send()


def local(hidden_in, w_up, w_down, norm_gain, title_length, label_leaf, leaf_parent):
    ny, nz, nc = (lax.axis_size(a) for a in LABELS)
    plane = ny * nc
    vmem, dma = pltpu.VMEM, pltpu.SemaphoreType.DMA
    in_vmem = pl.BlockSpec(memory_space=pltpu.VMEM)
    anywhere = pl.BlockSpec(memory_space=pl.ANY)
    gather = vmem((PIECES, 64, 2 * SHARE), BF16)
    near = vmem((PIECES, 16, WIDE), BF16)
    scattered = vmem((PIECES, 2, 16, WIDE), BF16)
    pair = dma((2, PIECES))
    return pl.pallas_call(
        functools.partial(kernel, ny, nz, nc),
        out_shape=(
            jax.ShapeDtypeStruct((LAB, WIDE), BF16),
            jax.ShapeDtypeStruct((LEAF, SHARE), F32),
            jax.ShapeDtypeStruct((PAR, SHARE), F32),
        ),
        in_specs=[
            pl.BlockSpec(memory_space=pltpu.SMEM),
            anywhere, anywhere, anywhere, in_vmem, in_vmem, in_vmem,
        ],
        out_specs=(in_vmem,) * 3,
        scratch_shapes=[
            vmem((NX * 128, SHARE), BF16),
            gather,
            vmem((NX, SHARE, WIDE), BF16),
            vmem((WIDE, WIDE), BF16),
            gather, gather, gather,
            vmem((PIECES, NX, 2, 16, WIDE), BF16),
            near, near, scattered, scattered,
            vmem((NX, 128, SHARE), BF16),
            vmem((8, 128), jnp.int32),
            vmem((plane, 8, 128), jnp.int32),
            vmem((nz * LEAF, plane * LAB), F32),
            vmem((nz * PAR, plane * LEAF), F32),
            vmem((NX, 8, PAD), BF16),
            vmem((plane * NX, 8, PAD), BF16),
            vmem((NX, NX, 8, PAD), BF16),
            vmem((nz, LEAF, PAD), BF16),
            vmem((nz, LEAF, PAD), BF16),
            vmem((LEAF, PAD), F32),
            vmem((plane, LEAF, PAD), F32),
            vmem((NX, plane, LEAF, 128), F32),
            vmem((nz, PAR, PAD), F32),
            vmem((nz, PAR, PAD), F32),
            dma((2 + NX,)),
            pair, pair, pair, pair, pair, pair, pair, pair,
            dma(()), dma(()), dma(()), dma(()),
            dma((NX,)), dma((NX,)),
            dma(()), dma(()), dma(()), dma(()), dma(()), dma(()), dma(()), dma(()),
        ],
        compiler_params=pltpu.CompilerParams(collective_id=0, has_side_effects=True),
    )(
        title_length,
        hidden_in,
        w_up,
        w_down,
        norm_gain[None, :],
        label_leaf[None, :],
        leaf_parent[None, :],
    )


def solution(mesh):
    labels = mesh.shape["labels"]
    side = 4 if labels == 128 else 2
    split = Mesh(
        mesh.devices.reshape(side, labels // side // 2, 2, mesh.shape["heads"]), (AY, AZ, AC, AX)
    )
    placed = (P(LABELS, AX), P(None, AX), P(AX, None), P(), P(LABELS), P(LABELS), P(LABELS))
    return jax.shard_map(
        local,
        mesh=split,
        in_specs=placed,
        out_specs=(P(LABELS, None), P(LABELS, AX), P(LABELS, AX)),
        check_vma=False,
    )
```

```python
import functools

import jax
import jax.numpy as jnp
from jax import lax
from jax.experimental import pallas as pl
from jax.experimental.pallas import tpu as pltpu
from jax.sharding import Mesh
from jax.sharding import PartitionSpec as P

AY, AZ, AC, AX = "labels_0", "labels_1", "labels_2", "heads"
LABELS = (AY, AZ, AC)
NX = 4
SEQ = 16
LAB = 32
LEAF = 8
PAR = 2
PIECES = 4
TOK = 128
OWN = TOK // NX
SHARE = 192
WIDE = 768
PAD = 256
MESH = pl.DeviceIdType.MESH
F32, BF16 = jnp.float32, jnp.bfloat16


def remote(src, dst, send, recv, **where):
    return pltpu.make_async_remote_copy(
        src_ref=src, dst_ref=dst, send_sem=send, recv_sem=recv, device_id=where, device_id_type=MESH
    )


def kernel(
    ny, nz, nc,
    len_ref, hidden, w_up, w_down, gain_ref, leaf_ref, parent_ref,
    embed_out, centers_out, sums_out,
    xg, xt, upv, downv, pb, rsr, table, tables, pick_leaf, pick_parent, blocks, lab, wide,
    zbuf, zrecv, sbuf, srecv, qrecv, pbuf, precv,
    near_y, far_y, other_c, hops_z,
    local_sem, ag_send, ag_recv, rs_send, rs_recv,
    t_send, t_recv, s1_send, s1_recv, e_send, e_recv, z1_send, z1_recv,
    s2_send, s2_recv, q_send, q_recv, z2_send, z2_recv,
):
    y, z, c, x = (lax.axis_index(a) for a in (AY, AZ, AC, AX))
    plane = ny * nc
    here = y * nc + c
    right = {AX: lax.rem(x + 1, NX)}
    mates = [
        (lax.rem(y + dy, ny), lax.rem(c + dc, nc))
        for dy in sorted(range(ny), key=lambda d: -min(d, ny - d))
        for dc in reversed(range(nc))
    ]
    z_order = sorted(range(1, nz), key=lambda k: -min(k, nz - k))
    x_order = (2, 1, 3, 0)
    drain = []

    def signal(sem, **where):
        pl.semaphore_signal(sem, 1, device_id=where, device_id_type=MESH)

    def around(axis, at, size, step, sem):
        signal(sem, **{axis: lax.rem(at + step, size)})
        signal(sem, **{axis: lax.rem(at + size - step, size)})

    barrier = pltpu.get_barrier_semaphore()
    for k in (2, 1, 3):
        signal(barrier, **{AX: lax.rem(x + k, NX)})
    around(AY, y, ny, 1, barrier)
    around(AZ, z, nz, 1, barrier)
    signal(barrier, **{AC: 1 - c})
    loads = []
    for p in range(PIECES):
        cols = hidden.at[:, pl.ds(TOK * p, TOK)]
        loads.append(pltpu.make_async_copy(cols, xg.at[p, x], local_sem.at[p]))
    loads.append(pltpu.make_async_copy(w_up, upv, local_sem.at[PIECES]))
    loads.append(pltpu.make_async_copy(w_down, downv, local_sem.at[PIECES + 1]))
    for load in loads:
        load.start()
    pl.semaphore_wait(barrier, 8)

    ag = []
    for p in range(PIECES):
        for k in (2, 1, 3):
            cols = hidden.at[:, pl.ds(TOK * p, TOK)]
            to = {AX: lax.rem(x + k, NX)}
            ag.append(remote(cols, xg.at[p, x], ag_send.at[p, k], ag_recv.at[p, k], **to))
            ag[-1].start()
            drain.append(ag[-1].wait_send)

    around(AY, y, ny, 1, near_y)
    steps = [s for s in (1, 2, 4) if 2 * s <= nz // 2]
    if steps:
        around(AZ, z, nz, steps[0], hops_z.at[0])

    def handshake_2():
        pl.semaphore_wait(near_y, 2)
        around(AY, y, ny, 1, far_y)
        if len(steps) > 0:
            pl.semaphore_wait(hops_z.at[0], 2)
        if len(steps) > 1:
            around(AZ, z, nz, steps[1], hops_z.at[1])

    def handshake_3():
        pl.semaphore_wait(far_y, 2)
        signal(other_c, **{AC: 1 - c})
        if len(steps) > 1:
            pl.semaphore_wait(hops_z.at[1], 2)
        if len(steps) > 2:
            around(AZ, z, nz, steps[2], hops_z.at[2])

    def handshake_4():
        pl.semaphore_wait(other_c, 1)
        if len(steps) > 2:
            pl.semaphore_wait(hops_z.at[2], 2)

    row = lax.broadcasted_iota(jnp.int32, (LAB, LAB), 0)
    col = lax.broadcasted_iota(jnp.int32, (LAB, LAB), 1)
    inner = lax.rem(col, 8)
    natural = 8 * lax.div(inner, 2) + 2 * lax.div(col, 8) + lax.rem(inner, 2)
    leaves = jnp.broadcast_to(leaf_ref[...], (8, LAB)).astype(F32)
    ordered = jnp.dot(
        leaves, (row == natural).astype(F32), preferred_element_type=F32, precision=lax.Precision.HIGHEST
    )
    table[...] = jnp.zeros_like(table)
    table[0:1, 0:LAB] = ordered[0:1].astype(jnp.int32)
    table[1:2, 0:LEAF] = parent_ref[...]

    rs = {}

    def compute(p):
        features = xg[p].reshape(WIDE, TOK).T
        xt[p] = features
        upward = jnp.dot(features, upv[...], preferred_element_type=F32)
        activ = (0.5 * upward * (1.0 + lax.erf(upward * (0.5**0.5)))).astype(BF16)
        partial = jnp.dot(activ, downv[...], preferred_element_type=F32).astype(BF16)
        for j in range(NX):
            pb[p, j] = partial[OWN * j : OWN * (j + 1)]
        for k in (2, 1, 3):
            to = lax.rem(x + k, NX)
            rs[p, k] = remote(pb.at[p, to], rsr.at[p, k - 1], rs_send.at[p, k], rs_recv.at[p, k], **{AX: to})
            rs[p, k].start()
            drain.append(rs[p, k].wait_send)

    for load in loads:
        load.wait()
    for p in range(PIECES):
        for copy in ag[3 * p : 3 * p + 3]:
            copy.wait_recv()
        compute(p)
        if p == 0:
            handshake_2()
        if p == 2:
            handshake_3()
    handshake_4()

    for yy, cc in mates[:-1]:
        remote(table, tables.at[here], t_send, t_recv, **{AY: yy, AC: cc}).start()
    tables[here] = table[...]

    gain = gain_ref[...].reshape(1, WIDE)
    position = lax.broadcasted_iota(jnp.int32, (SEQ, 1), 0)
    embeds = []

    def pool(p):
        for k in (2, 1, 3):
            rs[p, k].wait_recv()
        for half in range(2):
            rows = pl.ds(pl.multiple_of(OWN * x + SEQ * half, SEQ), SEQ)
            there = pl.ds(SEQ * half, SEQ)
            summed = pb[p, x, there].astype(F32)
            for k in range(NX - 1):
                summed = summed + rsr[p, k, there].astype(F32)
            mixed = (xt[p, rows].astype(F32) + summed).astype(BF16).astype(F32)
            mean = jnp.mean(mixed, axis=1, keepdims=True)
            centred = mixed - mean
            variance = jnp.mean(centred * centred, axis=1, keepdims=True)
            normed = centred * lax.rsqrt(variance + 1e-05) * gain
            length = len_ref[8 * p + 2 * x + half]
            kept = jnp.where(position < length, normed, 0.0)
            pooled = jnp.sum(kept, axis=0, keepdims=True) / length.astype(F32)
            embeds.append(pooled * lax.rsqrt(jnp.mean(pooled * pooled, axis=1, keepdims=True) + 1e-05))

    for p in range(PIECES):
        pool(p)
    embed = jnp.concatenate(embeds, axis=0)
    zero = jnp.zeros((8, PAD - SHARE), F32)
    for s in range(NX):
        part = embed[:, SHARE * s : SHARE * (s + 1)]
        blocks[s] = jnp.concatenate([part, zero], axis=1).astype(BF16)

    slot = here * NX + x
    for n, (yy, cc) in enumerate(mates):
        for k in x_order:
            if k == 0 and n == plane - 1:
                continue
            to = lax.rem(x + k, NX)
            remote(blocks.at[to], lab.at[slot], s1_send, s1_recv, **{AY: yy, AC: cc, AX: to}).start()
    spread = []
    for k in (2, 1, 3):
        to = {AX: lax.rem(x + k, NX)}
        spread.append(remote(blocks, wide.at[x], e_send.at[k], e_recv.at[k], **to))
        spread[-1].start()
        drain.append(spread[-1].wait_send)
    lab[slot] = blocks[x]
    wide[x] = blocks[...]

    others = tables.at[pl.ds(0, plane - 1)]
    others = remote(others, others, t_send, t_recv, **right)
    others.wait_recv()
    drain.append(others.wait_send)
    column = nz * LEAF
    row = lax.broadcasted_iota(jnp.int32, (column, 1), 0)
    leaf_of_row = ((y * nz + lax.div(row, LEAF)) * nc + c) * LEAF + lax.rem(row, LEAF)
    row2 = lax.broadcasted_iota(jnp.int32, (nz * PAR, 1), 0)
    parent_of_row = ((y * nz + lax.div(row2, PAR)) * nc + c) * PAR + lax.rem(row2, PAR)
    for k in range(plane):
        pick_leaf[:, LAB * k : LAB * (k + 1)] = (leaf_of_row == tables[k, 0:1, 0:LAB]).astype(F32)
        pick = (parent_of_row == tables[k, 1:2, 0:LEAF]).astype(F32)
        for part in range(3):
            first = (plane * part + k) * LEAF
            pick_parent[:, first : first + LEAF] = pick
    picked_leaf = pick_leaf[...].astype(BF16)

    got = lab.at[pl.ds(0, plane * NX - 1)]
    got = remote(got, got, s1_send, s1_recv, **right)
    drain.append(got.wait_send)
    got.wait_recv()
    labels = lab[...].astype(F32).reshape(plane * LAB, PAD).astype(BF16)
    leaf_part = jnp.dot(picked_leaf, labels, preferred_element_type=F32)
    zbuf[...] = leaf_part.reshape(nz, LEAF, PAD).astype(BF16)
    for k in z_order:
        to = lax.rem(z + k, nz)
        remote(zbuf.at[to], zrecv.at[z], z1_send, z1_recv, **{AZ: to}).start()
    zrecv[z] = zbuf[z]

    for copy in spread:
        copy.wait_recv()
    whole = [
        jnp.concatenate([wide[s, b].astype(F32)[:, :SHARE] for b in range(NX)], axis=1) for s in range(NX)
    ]
    embed_out[...] = jnp.concatenate(
        [whole[s][2 * p : 2 * p + 2] for p in range(PIECES) for s in range(NX)], axis=0
    ).astype(BF16)

    got = zrecv.at[pl.ds(0, nz - 1)]
    got = remote(got, got, z1_send, z1_recv, **right)
    drain.append(got.wait_send)
    got.wait_recv()
    leaf_sum = jnp.sum(zrecv[...].astype(F32), axis=0)
    square = jnp.sum(leaf_sum * leaf_sum, axis=1, keepdims=True)
    lane = lax.broadcasted_iota(jnp.int32, (LEAF, PAD), 1)
    sbuf[...] = jnp.where(lane < SHARE, leaf_sum, square)

    for n, (yy, cc) in enumerate(mates):
        for k in x_order:
            to = {AY: yy, AC: cc, AX: lax.rem(x + k, NX)}
            if k > 0:
                remote(sbuf.at[:, pl.ds(128, 128)], qrecv.at[x, here], q_send, q_recv, **to).start()
            elif n < plane - 1:
                remote(sbuf, srecv.at[here], s2_send, s2_recv, **to).start()
    srecv[here] = sbuf[...]
    qrecv[x] = jnp.zeros_like(qrecv[x])
    got = srecv.at[pl.ds(0, plane - 1)]
    got = remote(got, got, s2_send, s2_recv, **right)
    drain.append(got.wait_send)
    got.wait_recv()
    got = qrecv.at[pl.ds(0, NX - 1)]
    got = remote(got, got, q_send, q_recv, **right)
    drain.append(got.wait_send)
    got.wait_recv()
    sums = srecv[...]
    total = sums[:, :, PAD - 1 :] + jnp.sum(qrecv[...], axis=0)[:, :, 127:]
    centers = (sums * lax.rsqrt(total / WIDE + 1e-05)).reshape(plane * LEAF, PAD)
    parts = []
    rest = centers
    for part in range(3):
        parts.append(rest.astype(BF16))
        rest = rest - parts[-1].astype(F32)
    parent_part = jnp.dot(
        pick_parent[...].astype(BF16), jnp.concatenate(parts, axis=0), preferred_element_type=F32
    )
    for k in range(nz):
        pbuf[k] = parent_part[PAR * k : PAR * (k + 1)]
    for k in z_order:
        to = lax.rem(z + k, nz)
        remote(pbuf.at[to], precv.at[z], z2_send, z2_recv, **{AZ: to}).start()
    precv[z] = pbuf[z]
    mine = srecv[here]
    total = mine[:, PAD - 1 :]
    for s in range(NX):
        total = total + qrecv[s, here][:, 127:]
    centers_out[...] = (mine * lax.rsqrt(total / WIDE + 1e-05))[:, :SHARE]
    got = precv.at[pl.ds(0, nz - 1)]
    got = remote(got, got, z2_send, z2_recv, **right)
    drain.append(got.wait_send)
    got.wait_recv()
    sums_out[...] = jnp.sum(precv[...], axis=0)[:, :SHARE]
    for wait in drain:
        wait()


def hand_over(*refs):
    ins, outs, sem = refs[:3], refs[3:6], refs[6]
    copies = [pltpu.make_async_copy(a, b, sem.at[i]) for i, (a, b) in enumerate(zip(ins, outs))]
    for copy in copies:
        copy.start()
    for copy in copies:
        copy.wait()


def local(hidden_in, w_up, w_down, norm_gain, title_length, label_leaf, leaf_parent):
    ny, nz, nc = (lax.axis_size(a) for a in LABELS)
    plane = ny * nc
    vmem, dma, regular = pltpu.VMEM, pltpu.SemaphoreType.DMA, pltpu.SemaphoreType.REGULAR
    in_vmem = pl.BlockSpec(memory_space=pltpu.VMEM)
    anywhere = pl.BlockSpec(memory_space=pl.ANY)
    out_shape = (
        jax.ShapeDtypeStruct((LAB, WIDE), BF16),
        jax.ShapeDtypeStruct((LEAF, SHARE), F32),
        jax.ShapeDtypeStruct((PAR, SHARE), F32),
    )
    outs = pl.pallas_call(
        functools.partial(kernel, ny, nz, nc),
        out_shape=out_shape,
        in_specs=[
            pl.BlockSpec(memory_space=pltpu.SMEM),
            anywhere, anywhere, anywhere, in_vmem, in_vmem, in_vmem,
        ],
        out_specs=(in_vmem,) * 3,
        scratch_shapes=[
            vmem((PIECES, NX, SHARE, TOK), BF16),
            vmem((PIECES, TOK, WIDE), BF16),
            vmem((WIDE, WIDE), BF16),
            vmem((WIDE, WIDE), BF16),
            vmem((PIECES, NX, OWN, WIDE), BF16),
            vmem((PIECES, NX - 1, OWN, WIDE), BF16),
            vmem((8, 128), jnp.int32),
            vmem((plane, 8, 128), jnp.int32),
            vmem((nz * LEAF, plane * LAB), F32),
            vmem((nz * PAR, 3 * plane * LEAF), F32),
            vmem((NX, 8, PAD), BF16),
            vmem((plane * NX, 8, PAD), BF16),
            vmem((NX, NX, 8, PAD), BF16),
            vmem((nz, LEAF, PAD), BF16),
            vmem((nz, LEAF, PAD), BF16),
            vmem((LEAF, PAD), F32),
            vmem((plane, LEAF, PAD), F32),
            vmem((NX, plane, LEAF, 128), F32),
            vmem((nz, PAR, PAD), F32),
            vmem((nz, PAR, PAD), F32),
            regular, regular, regular, regular((3,)),
            dma((PIECES + 2,)),
            dma((PIECES, NX)), dma((PIECES, NX)), dma((PIECES, NX)), dma((PIECES, NX)),
            dma(()), dma(()), dma(()), dma(()),
            dma((NX,)), dma((NX,)),
            dma(()), dma(()), dma(()), dma(()), dma(()), dma(()), dma(()), dma(()),
        ],
        compiler_params=pltpu.CompilerParams(collective_id=0, has_side_effects=True),
    )(
        title_length,
        hidden_in.T,
        w_up,
        w_down,
        norm_gain,
        label_leaf[None, :],
        leaf_parent[None, :],
    )
    return pl.pallas_call(
        hand_over,
        out_shape=out_shape,
        in_specs=[anywhere] * 3,
        out_specs=(anywhere,) * 3,
        scratch_shapes=[dma((3,))],
    )(*outs)


def solution(mesh):
    labels = mesh.shape["labels"]
    side = 4 if labels == 128 else 2
    split = Mesh(
        mesh.devices.reshape(side, labels // side // 2, 2, mesh.shape["heads"]), (AY, AZ, AC, AX)
    )
    placed = (P(LABELS, AX), P(None, AX), P(AX, None), P(), P(LABELS), P(LABELS), P(LABELS))
    return jax.shard_map(
        local,
        mesh=split,
        in_specs=placed,
        out_specs=(P(LABELS, None), P(LABELS, AX), P(LABELS, AX)),
        check_vma=False,
    )
```

```python
import functools

import jax
import jax.numpy as jnp
from jax import lax
from jax.experimental import pallas as pl
from jax.experimental.pallas import tpu as pltpu
from jax.sharding import Mesh
from jax.sharding import PartitionSpec as P

AY, AZ, AC, AX = "labels_0", "labels_1", "labels_2", "heads"
LABELS = (AY, AZ, AC)
NX = 4
SEQ = 16
LAB = 32
LEAF = 8
PAR = 2
PIECES = 4
TOK = 128
OWN = TOK // NX
SHARE = 192
WIDE = 768
PAD = 256
MESH = pl.DeviceIdType.MESH
F32, BF16 = jnp.float32, jnp.bfloat16


def remote(src, dst, send, recv, **where):
    return pltpu.make_async_remote_copy(
        src_ref=src, dst_ref=dst, send_sem=send, recv_sem=recv, device_id=where, device_id_type=MESH
    )


def kernel(
    ny, nz, nc,
    len_ref, hidden, w_up, w_down, gain_ref, leaf_ref, parent_ref,
    embed_out, centers_out, sums_out,
    xg, xt, upv, downv, pb, rsr, table, tables, pick_leaf, pick_parent, blocks, lab, wide,
    zbuf, zrecv, sbuf, srecv, qrecv, pbuf, precv,
    near_y, far_y, other_c, hops_z,
    local_sem, ag_send, ag_recv, rs_send, rs_recv,
    t_send, t_recv, s1_send, s1_recv, e_send, e_recv, z1_send, z1_recv,
    s2_send, s2_recv, q_send, q_recv, z2_send, z2_recv,
):
    y, z, c, x = (lax.axis_index(a) for a in (AY, AZ, AC, AX))
    plane = ny * nc
    here = y * nc + c
    right = {AX: lax.rem(x + 1, NX)}
    mates = [
        (lax.rem(y + dy, ny), lax.rem(c + dc, nc))
        for dy in sorted(range(ny), key=lambda d: -min(d, ny - d))
        for dc in reversed(range(nc))
    ]
    z_order = sorted(range(1, nz), key=lambda k: -min(k, nz - k))
    x_order = (2, 1, 3, 0)
    drain = []

    def signal(sem, **where):
        pl.semaphore_signal(sem, 1, device_id=where, device_id_type=MESH)

    def around(axis, at, size, step, sem):
        signal(sem, **{axis: lax.rem(at + step, size)})
        signal(sem, **{axis: lax.rem(at + size - step, size)})

    barrier = pltpu.get_barrier_semaphore()
    for k in (2, 1, 3):
        signal(barrier, **{AX: lax.rem(x + k, NX)})
    around(AY, y, ny, 1, barrier)
    around(AZ, z, nz, 1, barrier)
    signal(barrier, **{AC: 1 - c})
    loads = []
    for p in range(PIECES):
        cols = hidden.at[:, pl.ds(TOK * p, TOK)]
        loads.append(pltpu.make_async_copy(cols, xg.at[p, x], local_sem.at[p]))
    loads.append(pltpu.make_async_copy(w_up, upv, local_sem.at[PIECES]))
    loads.append(pltpu.make_async_copy(w_down, downv, local_sem.at[PIECES + 1]))
    for load in loads:
        load.start()
    pl.semaphore_wait(barrier, 8)

    ag = []
    for p in range(PIECES):
        for k in (2, 1, 3):
            cols = hidden.at[:, pl.ds(TOK * p, TOK)]
            to = {AX: lax.rem(x + k, NX)}
            ag.append(remote(cols, xg.at[p, x], ag_send.at[p, k], ag_recv.at[p, k], **to))
            ag[-1].start()
            drain.append(ag[-1].wait_send)

    around(AY, y, ny, 1, near_y)
    steps = [s for s in (1, 2, 4) if 2 * s <= nz // 2]
    if steps:
        around(AZ, z, nz, steps[0], hops_z.at[0])

    def handshake_2():
        pl.semaphore_wait(near_y, 2)
        around(AY, y, ny, 1, far_y)
        if len(steps) > 0:
            pl.semaphore_wait(hops_z.at[0], 2)
        if len(steps) > 1:
            around(AZ, z, nz, steps[1], hops_z.at[1])

    def handshake_3():
        pl.semaphore_wait(far_y, 2)
        signal(other_c, **{AC: 1 - c})
        if len(steps) > 1:
            pl.semaphore_wait(hops_z.at[1], 2)
        if len(steps) > 2:
            around(AZ, z, nz, steps[2], hops_z.at[2])

    def handshake_4():
        pl.semaphore_wait(other_c, 1)
        if len(steps) > 2:
            pl.semaphore_wait(hops_z.at[2], 2)

    row = lax.broadcasted_iota(jnp.int32, (LAB, LAB), 0)
    col = lax.broadcasted_iota(jnp.int32, (LAB, LAB), 1)
    inner = lax.rem(col, 8)
    natural = 8 * lax.div(inner, 2) + 2 * lax.div(col, 8) + lax.rem(inner, 2)
    leaves = jnp.broadcast_to(leaf_ref[...], (8, LAB)).astype(F32)
    ordered = jnp.dot(
        leaves, (row == natural).astype(F32), preferred_element_type=F32, precision=lax.Precision.HIGHEST
    )
    table[...] = jnp.zeros_like(table)
    table[0:1, 0:LAB] = ordered[0:1].astype(jnp.int32)
    table[1:2, 0:LEAF] = parent_ref[...]

    rs = {}

    def compute(p):
        features = xg[p].reshape(WIDE, TOK).T
        xt[p] = features
        upward = jnp.dot(features, upv[...], preferred_element_type=F32)
        activ = (0.5 * upward * (1.0 + lax.erf(upward * (0.5**0.5)))).astype(BF16)
        partial = jnp.dot(activ, downv[...], preferred_element_type=F32).astype(BF16)
        for j in range(NX):
            pb[p, j] = partial[OWN * j : OWN * (j + 1)]
        for k in (2, 1, 3):
            to = lax.rem(x + k, NX)
            rs[p, k] = remote(pb.at[p, to], rsr.at[p, k - 1], rs_send.at[p, k], rs_recv.at[p, k], **{AX: to})
            rs[p, k].start()
            drain.append(rs[p, k].wait_send)

    for load in loads:
        load.wait()
    for p in range(PIECES):
        for copy in ag[3 * p : 3 * p + 3]:
            copy.wait_recv()
        compute(p)
        if p == 0:
            handshake_2()
        if p == 2:
            handshake_3()
    handshake_4()

    for yy, cc in mates[:-1]:
        remote(table, tables.at[here], t_send, t_recv, **{AY: yy, AC: cc}).start()
    tables[here] = table[...]

    gain = gain_ref[...].reshape(1, WIDE)
    position = lax.broadcasted_iota(jnp.int32, (SEQ, 1), 0)
    embeds = []

    def pool(p):
        for k in (2, 1, 3):
            rs[p, k].wait_recv()
        for half in range(2):
            rows = pl.ds(pl.multiple_of(OWN * x + SEQ * half, SEQ), SEQ)
            there = pl.ds(SEQ * half, SEQ)
            summed = pb[p, x, there].astype(F32)
            for k in range(NX - 1):
                summed = summed + rsr[p, k, there].astype(F32)
            mixed = (xt[p, rows].astype(F32) + summed).astype(BF16).astype(F32)
            mean = jnp.mean(mixed, axis=1, keepdims=True)
            centred = mixed - mean
            variance = jnp.mean(centred * centred, axis=1, keepdims=True)
            normed = centred * lax.rsqrt(variance + 1e-05) * gain
            length = len_ref[8 * p + 2 * x + half]
            kept = jnp.where(position < length, normed, 0.0)
            pooled = jnp.sum(kept, axis=0, keepdims=True) / length.astype(F32)
            embeds.append(pooled * lax.rsqrt(jnp.mean(pooled * pooled, axis=1, keepdims=True) + 1e-05))

    for p in range(PIECES):
        pool(p)
    embed = jnp.concatenate(embeds, axis=0)
    zero = jnp.zeros((8, PAD - SHARE), F32)
    for s in range(NX):
        part = embed[:, SHARE * s : SHARE * (s + 1)]
        blocks[s] = jnp.concatenate([part, zero], axis=1).astype(BF16)

    slot = here * NX + x
    for n, (yy, cc) in enumerate(mates):
        for k in x_order:
            if k == 0 and n == plane - 1:
                continue
            to = lax.rem(x + k, NX)
            remote(blocks.at[to], lab.at[slot], s1_send, s1_recv, **{AY: yy, AC: cc, AX: to}).start()
    spread = []
    for k in (2, 1, 3):
        to = {AX: lax.rem(x + k, NX)}
        spread.append(remote(blocks, wide.at[x], e_send.at[k], e_recv.at[k], **to))
        spread[-1].start()
        drain.append(spread[-1].wait_send)
    lab[slot] = blocks[x]
    wide[x] = blocks[...]

    others = tables.at[pl.ds(0, plane - 1)]
    others = remote(others, others, t_send, t_recv, **right)
    others.wait_recv()
    drain.append(others.wait_send)
    column = nz * LEAF
    row = lax.broadcasted_iota(jnp.int32, (column, 1), 0)
    leaf_of_row = ((y * nz + lax.div(row, LEAF)) * nc + c) * LEAF + lax.rem(row, LEAF)
    row2 = lax.broadcasted_iota(jnp.int32, (nz * PAR, 1), 0)
    parent_of_row = ((y * nz + lax.div(row2, PAR)) * nc + c) * PAR + lax.rem(row2, PAR)
    for k in range(plane):
        pick_leaf[:, LAB * k : LAB * (k + 1)] = (leaf_of_row == tables[k, 0:1, 0:LAB]).astype(F32)
        pick = (parent_of_row == tables[k, 1:2, 0:LEAF]).astype(F32)
        for part in range(3):
            first = (plane * part + k) * LEAF
            pick_parent[:, first : first + LEAF] = pick
    picked_leaf = pick_leaf[...].astype(BF16)

    got = lab.at[pl.ds(0, plane * NX - 1)]
    got = remote(got, got, s1_send, s1_recv, **right)
    drain.append(got.wait_send)
    got.wait_recv()
    labels = lab[...].astype(F32).reshape(plane * LAB, PAD).astype(BF16)
    leaf_part = jnp.dot(picked_leaf, labels, preferred_element_type=F32)
    zbuf[...] = leaf_part.reshape(nz, LEAF, PAD).astype(BF16)
    for k in z_order:
        to = lax.rem(z + k, nz)
        remote(zbuf.at[to], zrecv.at[z], z1_send, z1_recv, **{AZ: to}).start()
    zrecv[z] = zbuf[z]

    for copy in spread:
        copy.wait_recv()
    whole = [
        jnp.concatenate([wide[s, b].astype(F32)[:, :SHARE] for b in range(NX)], axis=1) for s in range(NX)
    ]
    embed_out[...] = jnp.concatenate(
        [whole[s][2 * p : 2 * p + 2] for p in range(PIECES) for s in range(NX)], axis=0
    ).astype(BF16)

    got = zrecv.at[pl.ds(0, nz - 1)]
    got = remote(got, got, z1_send, z1_recv, **right)
    drain.append(got.wait_send)
    got.wait_recv()
    leaf_sum = jnp.sum(zrecv[...].astype(F32), axis=0)
    square = jnp.sum(leaf_sum * leaf_sum, axis=1, keepdims=True)
    lane = lax.broadcasted_iota(jnp.int32, (LEAF, PAD), 1)
    sbuf[...] = jnp.where(lane < SHARE, leaf_sum, square)

    for n, (yy, cc) in enumerate(mates):
        for k in x_order:
            to = {AY: yy, AC: cc, AX: lax.rem(x + k, NX)}
            if k > 0:
                remote(sbuf.at[:, pl.ds(128, 128)], qrecv.at[x, here], q_send, q_recv, **to).start()
            elif n < plane - 1:
                remote(sbuf, srecv.at[here], s2_send, s2_recv, **to).start()
    srecv[here] = sbuf[...]
    qrecv[x] = jnp.zeros_like(qrecv[x])
    got = srecv.at[pl.ds(0, plane - 1)]
    got = remote(got, got, s2_send, s2_recv, **right)
    drain.append(got.wait_send)
    got.wait_recv()
    got = qrecv.at[pl.ds(0, NX - 1)]
    got = remote(got, got, q_send, q_recv, **right)
    drain.append(got.wait_send)
    got.wait_recv()
    sums = srecv[...]
    total = sums[:, :, PAD - 1 :] + jnp.sum(qrecv[...], axis=0)[:, :, 127:]
    centers = (sums * lax.rsqrt(total / WIDE + 1e-05)).reshape(plane * LEAF, PAD)
    parts = []
    rest = centers
    for part in range(3):
        parts.append(rest.astype(BF16))
        rest = rest - parts[-1].astype(F32)
    parent_part = jnp.dot(
        pick_parent[...].astype(BF16), jnp.concatenate(parts, axis=0), preferred_element_type=F32
    )
    for k in range(nz):
        pbuf[k] = parent_part[PAR * k : PAR * (k + 1)]
    for k in z_order:
        to = lax.rem(z + k, nz)
        remote(pbuf.at[to], precv.at[z], z2_send, z2_recv, **{AZ: to}).start()
    precv[z] = pbuf[z]
    mine = srecv[here]
    total = mine[:, PAD - 1 :]
    for s in range(NX):
        total = total + qrecv[s, here][:, 127:]
    centers_out[...] = (mine * lax.rsqrt(total / WIDE + 1e-05))[:, :SHARE]
    got = precv.at[pl.ds(0, nz - 1)]
    got = remote(got, got, z2_send, z2_recv, **right)
    drain.append(got.wait_send)
    got.wait_recv()
    sums_out[...] = jnp.sum(precv[...], axis=0)[:, :SHARE]
    for wait in drain:
        wait()


def hand_over(*refs):
    ins, outs = refs[:3], refs[3:6]
    for a, b in zip(ins, outs):
        b[...] = a[...]


def local(hidden_in, w_up, w_down, norm_gain, title_length, label_leaf, leaf_parent):
    ny, nz, nc = (lax.axis_size(a) for a in LABELS)
    plane = ny * nc
    vmem, dma, regular = pltpu.VMEM, pltpu.SemaphoreType.DMA, pltpu.SemaphoreType.REGULAR
    in_vmem = pl.BlockSpec(memory_space=pltpu.VMEM)
    anywhere = pl.BlockSpec(memory_space=pl.ANY)
    out_shape = (
        jax.ShapeDtypeStruct((LAB, WIDE), BF16),
        jax.ShapeDtypeStruct((LEAF, SHARE), F32),
        jax.ShapeDtypeStruct((PAR, SHARE), F32),
    )
    outs = pl.pallas_call(
        functools.partial(kernel, ny, nz, nc),
        out_shape=tuple(vmem(o.shape, o.dtype) for o in out_shape),
        in_specs=[
            pl.BlockSpec(memory_space=pltpu.SMEM),
            anywhere, anywhere, anywhere, in_vmem, in_vmem, in_vmem,
        ],
        out_specs=(in_vmem,) * 3,
        scratch_shapes=[
            vmem((PIECES, NX, SHARE, TOK), BF16),
            vmem((PIECES, TOK, WIDE), BF16),
            vmem((WIDE, WIDE), BF16),
            vmem((WIDE, WIDE), BF16),
            vmem((PIECES, NX, OWN, WIDE), BF16),
            vmem((PIECES, NX - 1, OWN, WIDE), BF16),
            vmem((8, 128), jnp.int32),
            vmem((plane, 8, 128), jnp.int32),
            vmem((nz * LEAF, plane * LAB), F32),
            vmem((nz * PAR, 3 * plane * LEAF), F32),
            vmem((NX, 8, PAD), BF16),
            vmem((plane * NX, 8, PAD), BF16),
            vmem((NX, NX, 8, PAD), BF16),
            vmem((nz, LEAF, PAD), BF16),
            vmem((nz, LEAF, PAD), BF16),
            vmem((LEAF, PAD), F32),
            vmem((plane, LEAF, PAD), F32),
            vmem((NX, plane, LEAF, 128), F32),
            vmem((nz, PAR, PAD), F32),
            vmem((nz, PAR, PAD), F32),
            regular, regular, regular, regular((3,)),
            dma((PIECES + 2,)),
            dma((PIECES, NX)), dma((PIECES, NX)), dma((PIECES, NX)), dma((PIECES, NX)),
            dma(()), dma(()), dma(()), dma(()),
            dma((NX,)), dma((NX,)),
            dma(()), dma(()), dma(()), dma(()), dma(()), dma(()), dma(()), dma(()),
        ],
        compiler_params=pltpu.CompilerParams(collective_id=0, has_side_effects=True),
    )(
        title_length,
        hidden_in.T,
        w_up,
        w_down,
        norm_gain,
        label_leaf[None, :],
        leaf_parent[None, :],
    )
    return pl.pallas_call(
        hand_over,
        out_shape=out_shape,
        in_specs=[in_vmem] * 3,
        out_specs=(in_vmem,) * 3,
    )(*(pltpu.with_memory_space_constraint(o, pltpu.VMEM) for o in outs))


def solution(mesh):
    labels = mesh.shape["labels"]
    side = 4 if labels == 128 else 2
    split = Mesh(
        mesh.devices.reshape(side, labels // side // 2, 2, mesh.shape["heads"]), (AY, AZ, AC, AX)
    )
    placed = (P(LABELS, AX), P(None, AX), P(AX, None), P(), P(LABELS), P(LABELS), P(LABELS))
    return jax.shard_map(
        local,
        mesh=split,
        in_specs=placed,
        out_specs=(P(LABELS, None), P(LABELS, AX), P(LABELS, AX)),
        check_vma=False,
    )
```

```python
import functools

import jax
import jax.numpy as jnp
from jax import lax
from jax.experimental import pallas as pl
from jax.experimental.pallas import tpu as pltpu
from jax.sharding import Mesh
from jax.sharding import PartitionSpec as P

AY, AZ, AC, AX = "labels_0", "labels_1", "labels_2", "heads"
LABELS = (AY, AZ, AC)
NX = 4
SEQ = 16
LAB = 32
LEAF = 8
PAR = 2
JOINED = (0, 1, 2)
PIECES = 4
TOK = 128
OWN = TOK // NX
SHARE = 192
WIDE = 768
PAD = 256
MESH = pl.DeviceIdType.MESH
F32, BF16 = jnp.float32, jnp.bfloat16


def remote(src, dst, send, recv, **where):
    return pltpu.make_async_remote_copy(
        src_ref=src, dst_ref=dst, send_sem=send, recv_sem=recv, device_id=where, device_id_type=MESH
    )


def kernel(
    ny, nz, nc,
    length_in, hidden, w_up, w_down, gain_in, leaf_in, parent_in,
    embed_out, centers_out, sums_out,
    len_ref, gain_ref, leaf_ref, parent_ref, xg, xt, upv, downv, pb, rsr, near, table, tables, pick_leaf, pick_parent, blocks, lab, wide,
    zbuf, zrecv, sbuf, srecv, qrecv, pbuf, precv,
    near_y, far_y, other_c, hops_z,
    local_sem, ag_send, ag_recv, rs_send, rs_recv, d2_send, d2_recv,
    n_send, n_recv, t_send, t_recv, s1_send, s1_recv, e_send, e_recv, z1_send, z1_recv,
    s2_send, s2_recv, q_send, q_recv, z2_send, z2_recv,
):
    y, z, c, x = (lax.axis_index(a) for a in (AY, AZ, AC, AX))
    plane = ny * nc
    here = y * nc + c
    right = {AX: lax.rem(x + 1, NX)}
    mates = [
        (lax.rem(y + dy, ny), lax.rem(c + dc, nc))
        for dy in sorted(range(ny), key=lambda d: -min(d, ny - d))
        for dc in reversed(range(nc))
    ]
    z_order = sorted(range(1, nz), key=lambda k: -min(k, nz - k))
    x_order = (2, 1, 3, 0)
    drain = []

    def signal(sem, **where):
        pl.semaphore_signal(sem, 1, device_id=where, device_id_type=MESH)

    def around(axis, at, size, step, sem):
        signal(sem, **{axis: lax.rem(at + step, size)})
        signal(sem, **{axis: lax.rem(at + size - step, size)})

    barrier = pltpu.get_barrier_semaphore()
    for k in (2, 1, 3):
        signal(barrier, **{AX: lax.rem(x + k, NX)})
    around(AY, y, ny, 1, barrier)
    around(AZ, z, nz, 1, barrier)
    signal(barrier, **{AC: 1 - c})
    loads = []
    for p in range(PIECES):
        cols = hidden.at[:, pl.ds(TOK * p, TOK)]
        loads.append(pltpu.make_async_copy(cols, xg.at[p, x], local_sem.at[p]))
    loads.append(pltpu.make_async_copy(w_up, upv, local_sem.at[PIECES]))
    loads.append(pltpu.make_async_copy(w_down, downv, local_sem.at[PIECES + 1]))
    small = [
        pltpu.make_async_copy(a, b, local_sem.at[PIECES + 2 + i])
        for i, (a, b) in enumerate(
            ((leaf_in, leaf_ref), (parent_in, parent_ref), (gain_in, gain_ref), (length_in, len_ref))
        )
    ]
    for load in small + loads:
        load.start()
    pl.semaphore_wait(barrier, 8)

    ag = []
    for p in range(PIECES):
        for k in (2, 1, 3):
            cols = hidden.at[:, pl.ds(TOK * p, TOK)]
            to = {AX: lax.rem(x + k, NX)}
            ag.append(remote(cols, xg.at[p, x], ag_send.at[p, k], ag_recv.at[p, k], **to))
            ag[-1].start()
            drain.append(ag[-1].wait_send)

    around(AY, y, ny, 1, near_y)
    steps = [s for s in (1, 2, 4) if 2 * s <= nz // 2]
    if steps:
        around(AZ, z, nz, steps[0], hops_z.at[0])

    def handshake_2():
        pl.semaphore_wait(near_y, 2)
        around(AY, y, ny, 1, far_y)
        if len(steps) > 0:
            pl.semaphore_wait(hops_z.at[0], 2)
        if len(steps) > 1:
            around(AZ, z, nz, steps[1], hops_z.at[1])

    def handshake_3():
        pl.semaphore_wait(far_y, 2)
        signal(other_c, **{AC: 1 - c})
        if len(steps) > 1:
            pl.semaphore_wait(hops_z.at[1], 2)
        if len(steps) > 2:
            around(AZ, z, nz, steps[2], hops_z.at[2])

    def handshake_4():
        pl.semaphore_wait(other_c, 1)
        if len(steps) > 2:
            pl.semaphore_wait(hops_z.at[2], 2)

    row = lax.broadcasted_iota(jnp.int32, (LAB, LAB), 0)
    col = lax.broadcasted_iota(jnp.int32, (LAB, LAB), 1)
    inner = lax.rem(col, 8)
    natural = 8 * lax.div(inner, 2) + 2 * lax.div(col, 8) + lax.rem(inner, 2)
    for load in small:
        load.wait()
    leaves = jnp.broadcast_to(leaf_ref[...], (8, LAB)).astype(F32)
    ordered = jnp.dot(
        leaves, (row == natural).astype(F32), preferred_element_type=F32, precision=lax.Precision.HIGHEST
    )
    table[...] = jnp.zeros_like(table)
    table[0:1, 0:LAB] = ordered[0:1].astype(jnp.int32)
    table[1:2, 0:LEAF] = parent_ref[...]

    joins, arrivals = {}, {}
    waits = []

    def compute(p):
        features = xg[p].reshape(WIDE, TOK).T
        xt[p] = features
        upward = jnp.dot(features, upv[...], preferred_element_type=F32)
        activ = (0.5 * upward * (1.0 + lax.erf(upward * (0.5**0.5)))).astype(BF16)
        partial = jnp.dot(activ, downv[...], preferred_element_type=F32).astype(BF16)
        for j in range(NX):
            pb[p, j] = partial[OWN * j : OWN * (j + 1)]
        if p in JOINED:
            join(p)
            return
        for k in (2, 1, 3):
            to = lax.rem(x + k, NX)
            launch(pb.at[p, to], rsr.at[p, k - 1], rs_send.at[p, k], rs_recv.at[p, k], to)

    low, high = pl.ds(0, SEQ), pl.ds(SEQ, SEQ)
    across = lax.rem(x + 2, NX)
    sides = tuple((k, lax.rem(x + k, NX), *rows) for k, rows in ((1, (low, high)), (3, (high, low))))

    def launch(src, dst, send, recv, to):
        copy = remote(src, dst, send, recv, **{AX: to})
        copy.start()
        drain.append(copy.wait_send)
        waits[0].append(copy.wait_recv)

    def join(p):
        n = JOINED.index(p)
        for k, to, through, plain in sides:
            joins[p, k] = remote(
                pb.at[p, across, through], near.at[n, through], d2_send.at[n, k], d2_recv.at[n, k], **{AX: to}
            )
            joins[p, k].start()
            drain.append(joins[p, k].wait_send)
        for k, to, through, plain in sides:
            launch(pb.at[p, to, plain], rsr.at[p, k - 1, plain], n_send.at[n, k], n_recv.at[n, k], to)

    def finish(p):
        n = JOINED.index(p)
        for k, to, through, plain in sides:
            joins[p, k].wait_recv()
            both = pb[p, to, through].astype(F32) + near[n, through].astype(F32)
            pb[p, to, through] = both.astype(BF16)
            launch(pb.at[p, to, through], rsr.at[p, k - 1, through], rs_send.at[p, k], rs_recv.at[p, k], to)

    for load in loads:
        load.wait()
    for p in range(PIECES):
        for copy in ag[3 * p : 3 * p + 3]:
            copy.wait_recv()
        waits[:] = [arrivals.setdefault(p, [])]
        compute(p)
        if p == 0:
            handshake_2()
        if p == 2:
            handshake_3()
    for p in JOINED:
        waits[:] = [arrivals[p]]
        finish(p)
    handshake_4()

    for yy, cc in mates[:-1]:
        remote(table, tables.at[here], t_send, t_recv, **{AY: yy, AC: cc}).start()
    tables[here] = table[...]

    gain = gain_ref[...].reshape(1, WIDE)
    position = lax.broadcasted_iota(jnp.int32, (SEQ, 1), 0)
    embeds = {}

    def pool(p):
        for wait in arrivals[p]:
            wait()
        for half in range(2):
            rows = pl.ds(pl.multiple_of(OWN * x + SEQ * half, SEQ), SEQ)
            there = pl.ds(SEQ * half, SEQ)
            summed = pb[p, x, there].astype(F32)
            for k in (0, 2) if p in JOINED else range(NX - 1):
                summed = summed + rsr[p, k, there].astype(F32)
            mixed = (xt[p, rows].astype(F32) + summed).astype(BF16).astype(F32)
            mean = jnp.mean(mixed, axis=1, keepdims=True)
            centred = mixed - mean
            variance = jnp.mean(centred * centred, axis=1, keepdims=True)
            normed = centred * lax.rsqrt(variance + 1e-05) * gain
            length = len_ref[8 * p + 2 * x + half]
            kept = jnp.where(position < length, normed, 0.0)
            pooled = jnp.sum(kept, axis=0, keepdims=True) / length.astype(F32)
            scale = lax.rsqrt(jnp.mean(pooled * pooled, axis=1, keepdims=True) + 1e-05)
            embeds[p, half] = pooled * scale

    for p in (0, 3, 1, 2):
        pool(p)
    embed = jnp.concatenate([embeds[p, half] for p in range(PIECES) for half in range(2)], axis=0)
    zero = jnp.zeros((8, PAD - SHARE), F32)
    for s in range(NX):
        part = embed[:, SHARE * s : SHARE * (s + 1)]
        blocks[s] = jnp.concatenate([part, zero], axis=1).astype(BF16)

    slot = here * NX + x
    for n, (yy, cc) in enumerate(mates):
        for k in x_order:
            if k == 0 and n == plane - 1:
                continue
            to = lax.rem(x + k, NX)
            remote(blocks.at[to], lab.at[slot], s1_send, s1_recv, **{AY: yy, AC: cc, AX: to}).start()
    lab[slot] = blocks[x]
    wide[x] = blocks[...]

    others = tables.at[pl.ds(0, plane - 1)]
    others = remote(others, others, t_send, t_recv, **right)
    others.wait_recv()
    drain.append(others.wait_send)
    column = nz * LEAF
    row = lax.broadcasted_iota(jnp.int32, (column, 1), 0)
    leaf_of_row = ((y * nz + lax.div(row, LEAF)) * nc + c) * LEAF + lax.rem(row, LEAF)
    row2 = lax.broadcasted_iota(jnp.int32, (nz * PAR, 1), 0)
    parent_of_row = ((y * nz + lax.div(row2, PAR)) * nc + c) * PAR + lax.rem(row2, PAR)
    for k in range(plane):
        pick_leaf[:, LAB * k : LAB * (k + 1)] = (leaf_of_row == tables[k, 0:1, 0:LAB]).astype(F32)
        pick = (parent_of_row == tables[k, 1:2, 0:LEAF]).astype(F32)
        for part in range(3):
            first = (plane * part + k) * LEAF
            pick_parent[:, first : first + LEAF] = pick
    picked_leaf = pick_leaf[...].astype(BF16)

    got = lab.at[pl.ds(0, plane * NX - 1)]
    got = remote(got, got, s1_send, s1_recv, **right)
    drain.append(got.wait_send)
    got.wait_recv()
    labels = lab[...].astype(F32).reshape(plane * LAB, PAD).astype(BF16)
    leaf_part = jnp.dot(picked_leaf, labels, preferred_element_type=F32)
    zbuf[...] = leaf_part.reshape(nz, LEAF, PAD).astype(BF16)
    for k in z_order:
        to = lax.rem(z + k, nz)
        remote(zbuf.at[to], zrecv.at[z], z1_send, z1_recv, **{AZ: to}).start()
    zrecv[z] = zbuf[z]
    spread = []
    for k in (2, 1, 3):
        to = {AX: lax.rem(x + k, NX)}
        spread.append(remote(blocks, wide.at[x], e_send.at[k], e_recv.at[k], **to))
        spread[-1].start()
        drain.append(spread[-1].wait_send)

    for copy in spread:
        copy.wait_recv()
    whole = [
        jnp.concatenate([wide[s, b].astype(F32)[:, :SHARE] for b in range(NX)], axis=1) for s in range(NX)
    ]
    embed_out[...] = jnp.concatenate(
        [whole[s][2 * p : 2 * p + 2] for p in range(PIECES) for s in range(NX)], axis=0
    ).astype(BF16)

    got = zrecv.at[pl.ds(0, nz - 1)]
    got = remote(got, got, z1_send, z1_recv, **right)
    drain.append(got.wait_send)
    got.wait_recv()
    leaf_sum = jnp.sum(zrecv[...].astype(F32), axis=0)
    square = jnp.sum(leaf_sum * leaf_sum, axis=1, keepdims=True)
    lane = lax.broadcasted_iota(jnp.int32, (LEAF, PAD), 1)
    sbuf[...] = jnp.where(lane < SHARE, leaf_sum, square)

    for n, (yy, cc) in enumerate(mates):
        for k in x_order:
            to = {AY: yy, AC: cc, AX: lax.rem(x + k, NX)}
            if k > 0:
                remote(sbuf.at[:, pl.ds(128, 128)], qrecv.at[x, here], q_send, q_recv, **to).start()
            elif n < plane - 1:
                remote(sbuf, srecv.at[here], s2_send, s2_recv, **to).start()
    srecv[here] = sbuf[...]
    qrecv[x] = jnp.zeros_like(qrecv[x])
    got = srecv.at[pl.ds(0, plane - 1)]
    got = remote(got, got, s2_send, s2_recv, **right)
    drain.append(got.wait_send)
    got.wait_recv()
    got = qrecv.at[pl.ds(0, NX - 1)]
    got = remote(got, got, q_send, q_recv, **right)
    drain.append(got.wait_send)
    got.wait_recv()
    sums = srecv[...]
    total = sums[:, :, PAD - 1 :] + jnp.sum(qrecv[...], axis=0)[:, :, 127:]
    centers = (sums * lax.rsqrt(total / WIDE + 1e-05)).reshape(plane * LEAF, PAD)
    parts = []
    rest = centers
    for part in range(3):
        parts.append(rest.astype(BF16))
        rest = rest - parts[-1].astype(F32)
    parent_part = jnp.dot(
        pick_parent[...].astype(BF16), jnp.concatenate(parts, axis=0), preferred_element_type=F32
    )
    for k in range(nz):
        pbuf[k] = parent_part[PAR * k : PAR * (k + 1)]
    for k in z_order:
        to = lax.rem(z + k, nz)
        remote(pbuf.at[to], precv.at[z], z2_send, z2_recv, **{AZ: to}).start()
    precv[z] = pbuf[z]
    mine = srecv[here]
    total = mine[:, PAD - 1 :]
    for s in range(NX):
        total = total + qrecv[s, here][:, 127:]
    centers_out[...] = (mine * lax.rsqrt(total / WIDE + 1e-05))[:, :SHARE]
    got = precv.at[pl.ds(0, nz - 1)]
    got = remote(got, got, z2_send, z2_recv, **right)
    drain.append(got.wait_send)
    got.wait_recv()
    sums_out[...] = jnp.sum(precv[...], axis=0)[:, :SHARE]
    for wait in drain:
        wait()


def hand_over(*refs):
    ins, outs = refs[:3], refs[3:6]
    for a, b in zip(ins, outs):
        b[...] = a[...]


def local(hidden_in, w_up, w_down, norm_gain, title_length, label_leaf, leaf_parent):
    ny, nz, nc = (lax.axis_size(a) for a in LABELS)
    plane = ny * nc
    vmem, dma, regular = pltpu.VMEM, pltpu.SemaphoreType.DMA, pltpu.SemaphoreType.REGULAR
    in_vmem = pl.BlockSpec(memory_space=pltpu.VMEM)
    anywhere = pl.BlockSpec(memory_space=pl.ANY)
    out_shape = (
        jax.ShapeDtypeStruct((LAB, WIDE), BF16),
        jax.ShapeDtypeStruct((LEAF, SHARE), F32),
        jax.ShapeDtypeStruct((PAR, SHARE), F32),
    )
    outs = pl.pallas_call(
        functools.partial(kernel, ny, nz, nc),
        out_shape=tuple(vmem(o.shape, o.dtype) for o in out_shape),
        in_specs=[anywhere] * 7,
        out_specs=(in_vmem,) * 3,
        scratch_shapes=[
            pltpu.SMEM((LAB,), jnp.int32),
            vmem((WIDE,), F32),
            vmem((1, LAB), jnp.int32),
            vmem((1, LEAF), jnp.int32),
            vmem((PIECES, NX, SHARE, TOK), BF16),
            vmem((PIECES, TOK, WIDE), BF16),
            vmem((WIDE, WIDE), BF16),
            vmem((WIDE, WIDE), BF16),
            vmem((PIECES, NX, OWN, WIDE), BF16),
            vmem((PIECES, NX - 1, OWN, WIDE), BF16),
            vmem((len(JOINED), OWN, WIDE), BF16),
            vmem((8, 128), jnp.int32),
            vmem((plane, 8, 128), jnp.int32),
            vmem((nz * LEAF, plane * LAB), F32),
            vmem((nz * PAR, 3 * plane * LEAF), F32),
            vmem((NX, 8, PAD), BF16),
            vmem((plane * NX, 8, PAD), BF16),
            vmem((NX, NX, 8, PAD), BF16),
            vmem((nz, LEAF, PAD), BF16),
            vmem((nz, LEAF, PAD), BF16),
            vmem((LEAF, PAD), F32),
            vmem((plane, LEAF, PAD), F32),
            vmem((NX, plane, LEAF, 128), F32),
            vmem((nz, PAR, PAD), F32),
            vmem((nz, PAR, PAD), F32),
            regular, regular, regular, regular((3,)),
            dma((PIECES + 6,)),
            dma((PIECES, NX)), dma((PIECES, NX)), dma((PIECES, NX)), dma((PIECES, NX)),
            dma((3, NX)), dma((3, NX)), dma((3, NX)), dma((3, NX)),
            dma(()), dma(()), dma(()), dma(()),
            dma((NX,)), dma((NX,)),
            dma(()), dma(()), dma(()), dma(()), dma(()), dma(()), dma(()), dma(()),
        ],
        compiler_params=pltpu.CompilerParams(collective_id=0, has_side_effects=True),
    )(
        title_length,
        hidden_in.T,
        w_up,
        w_down,
        norm_gain,
        label_leaf[None, :],
        leaf_parent[None, :],
    )
    return pl.pallas_call(
        hand_over,
        out_shape=out_shape,
        in_specs=[in_vmem] * 3,
        out_specs=(in_vmem,) * 3,
    )(*(pltpu.with_memory_space_constraint(o, pltpu.VMEM) for o in outs))


def solution(mesh):
    labels = mesh.shape["labels"]
    side = 4 if labels == 128 else 2
    split = Mesh(
        mesh.devices.reshape(side, labels // side // 2, 2, mesh.shape["heads"]), (AY, AZ, AC, AX)
    )
    placed = (P(LABELS, AX), P(None, AX), P(AX, None), P(), P(LABELS), P(LABELS), P(LABELS))
    return jax.shard_map(
        local,
        mesh=split,
        in_specs=placed,
        out_specs=(P(LABELS, None), P(LABELS, AX), P(LABELS, AX)),
        check_vma=False,
    )
```

```python
import functools

import jax
import jax.numpy as jnp
from jax import lax
from jax.experimental import pallas as pl
from jax.experimental.pallas import tpu as pltpu
from jax.sharding import Mesh
from jax.sharding import PartitionSpec as P

AY, AZ, AC, AX = "labels_0", "labels_1", "labels_2", "heads"
LABELS = (AY, AZ, AC)
NX = 4
SEQ = 16
LAB = 32
LEAF = 8
PAR = 2
PIECES = 4
ROLE = (2, 1, 3, 0)
TOK = 128
HALF, PART = TOK // 2, TOK // 4
SHARE = 192
WIDE = 768
PAD = 256
MESH = pl.DeviceIdType.MESH
F32, BF16 = jnp.float32, jnp.bfloat16


def remote(src, dst, send, recv, **where):
    return pltpu.make_async_remote_copy(
        src_ref=src, dst_ref=dst, send_sem=send, recv_sem=recv, device_id=where, device_id_type=MESH
    )


def kernel(
    ny, nz, nc,
    length_in, hidden, w_up, w_down, gain_in, leaf_in, parent_in,
    embed_out, centers_out, sums_out,
    len_ref, gain_ref, leaf_ref, parent_ref, xg, xt, upv, downv, pb, rsl, near, table, tables, pick_leaf, pick_parent, blocks, lab, wide,
    zbuf, zrecv, sbuf, srecv, qrecv, pbuf, precv,
    near_y, far_y, other_c, hops_z,
    local_sem, ag_send, ag_recv, rs_send, rs_recv, d2_send, d2_recv,
    t_send, t_recv, s1_send, s1_recv, e_send, e_recv, z1_send, z1_recv,
    s2_send, s2_recv, q_send, q_recv, z2_send, z2_recv,
):
    y, z, c, x = (lax.axis_index(a) for a in (AY, AZ, AC, AX))
    plane = ny * nc
    here = y * nc + c
    right = {AX: lax.rem(x + 1, NX)}
    mates = [
        (lax.rem(y + dy, ny), lax.rem(c + dc, nc))
        for dy in sorted(range(ny), key=lambda d: -min(d, ny - d))
        for dc in reversed(range(nc))
    ]
    z_order = sorted(range(1, nz), key=lambda k: -min(k, nz - k))
    x_order = (2, 1, 3, 0)
    drain = []

    def signal(sem, **where):
        pl.semaphore_signal(sem, 1, device_id=where, device_id_type=MESH)

    def around(axis, at, size, step, sem):
        signal(sem, **{axis: lax.rem(at + step, size)})
        signal(sem, **{axis: lax.rem(at + size - step, size)})

    barrier = pltpu.get_barrier_semaphore()
    for k in (2, 1, 3):
        signal(barrier, **{AX: lax.rem(x + k, NX)})
    around(AY, y, ny, 1, barrier)
    around(AZ, z, nz, 1, barrier)
    signal(barrier, **{AC: 1 - c})
    loads = []
    def piece_of(device, p):
        first = pl.multiple_of(lax.rem(device + ROLE[p], NX) * TOK, TOK)
        return hidden.at[:, pl.ds(first, TOK)]

    for p in range(PIECES):
        loads.append(pltpu.make_async_copy(piece_of(x, p), xg.at[p, x], local_sem.at[p]))
    loads.append(pltpu.make_async_copy(w_up, upv, local_sem.at[PIECES]))
    loads.append(pltpu.make_async_copy(w_down, downv, local_sem.at[PIECES + 1]))
    small = [
        pltpu.make_async_copy(a, b, local_sem.at[PIECES + 2 + i])
        for i, (a, b) in enumerate(
            ((leaf_in, leaf_ref), (parent_in, parent_ref), (gain_in, gain_ref), (length_in, len_ref))
        )
    ]
    for load in small + loads:
        load.start()
    pl.semaphore_wait(barrier, 8)

    ag = {}

    def gather(p):
        for k in (2, 1, 3):
            to = lax.rem(x + k, NX)
            copy = remote(piece_of(to, p), xg.at[p, x], ag_send.at[p, k], ag_recv.at[p, k], **{AX: to})
            copy.start()
            ag[p, k] = copy
            drain.append(copy.wait_send)

    for p in range(PIECES - 1):
        gather(p)

    around(AY, y, ny, 1, near_y)
    steps = [s for s in (1, 2, 4) if 2 * s <= nz // 2]
    if steps:
        around(AZ, z, nz, steps[0], hops_z.at[0])

    def handshake_2():
        pl.semaphore_wait(near_y, 2)
        around(AY, y, ny, 1, far_y)
        if len(steps) > 0:
            pl.semaphore_wait(hops_z.at[0], 2)
        if len(steps) > 1:
            around(AZ, z, nz, steps[1], hops_z.at[1])

    def handshake_3():
        pl.semaphore_wait(far_y, 2)
        signal(other_c, **{AC: 1 - c})
        if len(steps) > 1:
            pl.semaphore_wait(hops_z.at[1], 2)
        if len(steps) > 2:
            around(AZ, z, nz, steps[2], hops_z.at[2])

    def handshake_4():
        pl.semaphore_wait(other_c, 1)
        if len(steps) > 2:
            pl.semaphore_wait(hops_z.at[2], 2)

    for load in small:
        load.wait()
    table[...] = jnp.zeros_like(table)
    table[0:1, 0:LAB] = leaf_ref[...]
    table[1:2, 0:LEAF] = parent_ref[...]

    def compute(p):
        for k in (2, 1, 3):
            ag[p, k].wait_recv()
        features = xg[p].reshape(WIDE, TOK).T
        if p == PIECES - 1:
            xt[...] = features
        upward = jnp.dot(features, upv[...], preferred_element_type=F32)
        activ = (0.5 * upward * (1.0 + lax.erf(upward * (0.5**0.5)))).astype(BF16)
        pb[p] = jnp.dot(activ, downv[...], preferred_element_type=F32).astype(BF16)

    sides = ((0, 1, 0), (1, 3, HALF))
    joins, arrivals = {}, []

    def send(src, dst, send_sem, recv_sem, k):
        copy = remote(src, dst, send_sem, recv_sem, **{AX: lax.rem(x + k, NX)})
        copy.start()
        drain.append(copy.wait_send)
        return copy

    def finish(part):
        for side, k, first in sides:
            rows = pl.ds(first + PART * part, PART)
            joins[side, part].wait_recv()
            both = pb[1 + side, rows, :].astype(F32) + near[side, part].astype(F32)
            pb[1 + side, rows, :] = both.astype(BF16)
            arrivals.append(
                send(pb.at[1 + side, rows], rsl.at[side, rows], rs_send.at[side, part], rs_recv.at[side, part], k)
            )

    for load in loads:
        load.wait()
    compute(0)
    for part in range(2):
        for side, k, first in sides:
            rows = pl.ds(first + PART * part, PART)
            joins[side, part] = send(
                pb.at[0, rows], near.at[side, part], d2_send.at[side, part], d2_recv.at[side, part], k
            )
    gather(PIECES - 1)
    handshake_2()
    for side, k, first in sides:
        compute(1 + side)
        rows = pl.ds(HALF - first, HALF)
        arrivals.append(
            send(pb.at[1 + side, rows], rsl.at[side, rows], rs_send.at[side, 2], rs_recv.at[side, 2], k)
        )
    handshake_3()
    finish(0)
    finish(1)
    compute(PIECES - 1)
    handshake_4()

    for yy, cc in mates[:-1]:
        remote(table, tables.at[here], t_send, t_recv, **{AY: yy, AC: cc}).start()
    tables[here] = table[...]

    gain = gain_ref[...].reshape(1, WIDE)
    position = lax.broadcasted_iota(jnp.int32, (SEQ, 1), 0)
    embeds = {}

    def pool(label):
        rows = pl.ds(SEQ * label, SEQ)
        summed = pb[PIECES - 1, rows, :].astype(F32)
        for side in range(2):
            summed = summed + rsl[side, rows, :].astype(F32)
        mixed = (xt[rows, :].astype(F32) + summed).astype(BF16).astype(F32)
        mean = jnp.mean(mixed, axis=1, keepdims=True)
        centred = mixed - mean
        variance = jnp.mean(centred * centred, axis=1, keepdims=True)
        normed = centred * lax.rsqrt(variance + 1e-05) * gain
        length = len_ref[8 * x + label]
        kept = jnp.where(position < length, normed, 0.0)
        pooled = jnp.sum(kept, axis=0, keepdims=True) / length.astype(F32)
        embeds[label] = pooled * lax.rsqrt(jnp.mean(pooled * pooled, axis=1, keepdims=True) + 1e-05)

    for copies, group in ((arrivals[:4], (0, 1, 4, 5)), (arrivals[4:], (2, 3, 6, 7))):
        for copy in copies:
            copy.wait_recv()
        for label in group:
            pool(label)
    embed = jnp.concatenate([embeds[label] for label in range(8)], axis=0)
    zero = jnp.zeros((8, PAD - SHARE), F32)
    for s in range(NX):
        part = embed[:, SHARE * s : SHARE * (s + 1)]
        blocks[s] = jnp.concatenate([part, zero], axis=1).astype(BF16)

    slot = here * NX + x
    for n, (yy, cc) in enumerate(mates):
        for k in x_order:
            if k == 0 and n == plane - 1:
                continue
            to = lax.rem(x + k, NX)
            remote(blocks.at[to], lab.at[slot], s1_send, s1_recv, **{AY: yy, AC: cc, AX: to}).start()
    lab[slot] = blocks[x]
    wide[x] = blocks[...]

    others = tables.at[pl.ds(0, plane - 1)]
    others = remote(others, others, t_send, t_recv, **right)
    others.wait_recv()
    drain.append(others.wait_send)
    column = nz * LEAF
    row = lax.broadcasted_iota(jnp.int32, (column, 1), 0)
    leaf_of_row = ((y * nz + lax.div(row, LEAF)) * nc + c) * LEAF + lax.rem(row, LEAF)
    row2 = lax.broadcasted_iota(jnp.int32, (nz * PAR, 1), 0)
    parent_of_row = ((y * nz + lax.div(row2, PAR)) * nc + c) * PAR + lax.rem(row2, PAR)
    for k in range(plane):
        pick_leaf[:, LAB * k : LAB * (k + 1)] = (leaf_of_row == tables[k, 0:1, 0:LAB]).astype(F32)
        pick = (parent_of_row == tables[k, 1:2, 0:LEAF]).astype(F32)
        for part in range(3):
            first = (plane * part + k) * LEAF
            pick_parent[:, first : first + LEAF] = pick
    picked_leaf = pick_leaf[...].astype(BF16)

    got = lab.at[pl.ds(0, plane * NX - 1)]
    got = remote(got, got, s1_send, s1_recv, **right)
    drain.append(got.wait_send)
    got.wait_recv()
    labels = lab[...].astype(F32).reshape(plane * LAB, PAD).astype(BF16)
    leaf_part = jnp.dot(picked_leaf, labels, preferred_element_type=F32)
    zbuf[...] = leaf_part.reshape(nz, LEAF, PAD).astype(BF16)
    for k in z_order:
        to = lax.rem(z + k, nz)
        remote(zbuf.at[to], zrecv.at[z], z1_send, z1_recv, **{AZ: to}).start()
    zrecv[z] = zbuf[z]
    spread = []
    for k in (2, 1, 3):
        to = {AX: lax.rem(x + k, NX)}
        spread.append(remote(blocks, wide.at[x], e_send.at[k], e_recv.at[k], **to))
        spread[-1].start()
        drain.append(spread[-1].wait_send)

    for copy in spread:
        copy.wait_recv()
    whole = [
        jnp.concatenate([wide[s, b].astype(F32)[:, :SHARE] for b in range(NX)], axis=1) for s in range(NX)
    ]
    embed_out[...] = jnp.concatenate(whole, axis=0).astype(BF16)

    got = zrecv.at[pl.ds(0, nz - 1)]
    got = remote(got, got, z1_send, z1_recv, **right)
    drain.append(got.wait_send)
    got.wait_recv()
    leaf_sum = jnp.sum(zrecv[...].astype(F32), axis=0)
    square = jnp.sum(leaf_sum * leaf_sum, axis=1, keepdims=True)
    lane = lax.broadcasted_iota(jnp.int32, (LEAF, PAD), 1)
    sbuf[...] = jnp.where(lane < SHARE, leaf_sum, square)

    for n, (yy, cc) in enumerate(mates):
        for k in x_order:
            to = {AY: yy, AC: cc, AX: lax.rem(x + k, NX)}
            if k > 0:
                remote(sbuf.at[:, pl.ds(128, 128)], qrecv.at[x, here], q_send, q_recv, **to).start()
            elif n < plane - 1:
                remote(sbuf, srecv.at[here], s2_send, s2_recv, **to).start()
    srecv[here] = sbuf[...]
    qrecv[x] = jnp.zeros_like(qrecv[x])
    got = srecv.at[pl.ds(0, plane - 1)]
    got = remote(got, got, s2_send, s2_recv, **right)
    drain.append(got.wait_send)
    got.wait_recv()
    got = qrecv.at[pl.ds(0, NX - 1)]
    got = remote(got, got, q_send, q_recv, **right)
    drain.append(got.wait_send)
    got.wait_recv()
    sums = srecv[...]
    total = sums[:, :, PAD - 1 :] + jnp.sum(qrecv[...], axis=0)[:, :, 127:]
    centers = (sums * lax.rsqrt(total / WIDE + 1e-05)).reshape(plane * LEAF, PAD)
    parts = []
    rest = centers
    for part in range(3):
        parts.append(rest.astype(BF16))
        rest = rest - parts[-1].astype(F32)
    parent_part = jnp.dot(
        pick_parent[...].astype(BF16), jnp.concatenate(parts, axis=0), preferred_element_type=F32
    )
    for k in range(nz):
        pbuf[k] = parent_part[PAR * k : PAR * (k + 1)]
    for k in z_order:
        to = lax.rem(z + k, nz)
        remote(pbuf.at[to], precv.at[z], z2_send, z2_recv, **{AZ: to}).start()
    precv[z] = pbuf[z]
    mine = srecv[here]
    total = mine[:, PAD - 1 :]
    for s in range(NX):
        total = total + qrecv[s, here][:, 127:]
    centers_out[...] = (mine * lax.rsqrt(total / WIDE + 1e-05))[:, :SHARE]
    got = precv.at[pl.ds(0, nz - 1)]
    got = remote(got, got, z2_send, z2_recv, **right)
    drain.append(got.wait_send)
    got.wait_recv()
    sums_out[...] = jnp.sum(precv[...], axis=0)[:, :SHARE]
    for wait in drain:
        wait()


def hand_over(*refs):
    ins, outs = refs[:3], refs[3:6]
    for a, b in zip(ins, outs):
        b[...] = a[...]


def local(hidden_in, w_up, w_down, norm_gain, title_length, label_leaf, leaf_parent):
    ny, nz, nc = (lax.axis_size(a) for a in LABELS)
    plane = ny * nc
    vmem, dma, regular = pltpu.VMEM, pltpu.SemaphoreType.DMA, pltpu.SemaphoreType.REGULAR
    in_vmem = pl.BlockSpec(memory_space=pltpu.VMEM)
    anywhere = pl.BlockSpec(memory_space=pl.ANY)
    out_shape = (
        jax.ShapeDtypeStruct((LAB, WIDE), BF16),
        jax.ShapeDtypeStruct((LEAF, SHARE), F32),
        jax.ShapeDtypeStruct((PAR, SHARE), F32),
    )
    outs = pl.pallas_call(
        functools.partial(kernel, ny, nz, nc),
        out_shape=tuple(vmem(o.shape, o.dtype) for o in out_shape),
        in_specs=[anywhere] * 7,
        out_specs=(in_vmem,) * 3,
        scratch_shapes=[
            pltpu.SMEM((LAB,), jnp.int32),
            vmem((WIDE,), F32),
            vmem((1, LAB), jnp.int32),
            vmem((1, LEAF), jnp.int32),
            vmem((PIECES, NX, SHARE, TOK), BF16),
            vmem((TOK, WIDE), BF16),
            vmem((WIDE, WIDE), BF16),
            vmem((WIDE, WIDE), BF16),
            vmem((PIECES, TOK, WIDE), BF16),
            vmem((2, TOK, WIDE), BF16),
            vmem((2, 2, PART, WIDE), BF16),
            vmem((8, 128), jnp.int32),
            vmem((plane, 8, 128), jnp.int32),
            vmem((nz * LEAF, plane * LAB), F32),
            vmem((nz * PAR, 3 * plane * LEAF), F32),
            vmem((NX, 8, PAD), BF16),
            vmem((plane * NX, 8, PAD), BF16),
            vmem((NX, NX, 8, PAD), BF16),
            vmem((nz, LEAF, PAD), BF16),
            vmem((nz, LEAF, PAD), BF16),
            vmem((LEAF, PAD), F32),
            vmem((plane, LEAF, PAD), F32),
            vmem((NX, plane, LEAF, 128), F32),
            vmem((nz, PAR, PAD), F32),
            vmem((nz, PAR, PAD), F32),
            regular, regular, regular, regular((3,)),
            dma((PIECES + 6,)),
            dma((PIECES, NX)), dma((PIECES, NX)), dma((2, 3)), dma((2, 3)), dma((2, 2)), dma((2, 2)),
            dma(()), dma(()), dma(()), dma(()),
            dma((NX,)), dma((NX,)),
            dma(()), dma(()), dma(()), dma(()), dma(()), dma(()), dma(()), dma(()),
        ],
        compiler_params=pltpu.CompilerParams(collective_id=0, has_side_effects=True),
    )(
        title_length,
        hidden_in.T,
        w_up,
        w_down,
        norm_gain,
        label_leaf[None, :],
        leaf_parent[None, :],
    )
    return pl.pallas_call(
        hand_over,
        out_shape=out_shape,
        in_specs=[in_vmem] * 3,
        out_specs=(in_vmem,) * 3,
    )(*(pltpu.with_memory_space_constraint(o, pltpu.VMEM) for o in outs))


def solution(mesh):
    labels = mesh.shape["labels"]
    side = 4 if labels == 128 else 2
    split = Mesh(
        mesh.devices.reshape(side, labels // side // 2, 2, mesh.shape["heads"]), (AY, AZ, AC, AX)
    )
    placed = (P(LABELS, AX), P(None, AX), P(AX, None), P(), P(LABELS), P(LABELS), P(LABELS))
    return jax.shard_map(
        local,
        mesh=split,
        in_specs=placed,
        out_specs=(P(LABELS, None), P(LABELS, AX), P(LABELS, AX)),
        check_vma=False,
    )
```

```python
import functools

import jax
import jax.numpy as jnp
from jax import lax
from jax.experimental import pallas as pl
from jax.experimental.pallas import tpu as pltpu
from jax.sharding import Mesh
from jax.sharding import PartitionSpec as P

AY, AZ, AC, AX = "labels_0", "labels_1", "labels_2", "heads"
LABELS = (AY, AZ, AC)
NX = 4
SEQ = 16
LAB = 32
LEAF = 8
PAR = 2
PIECES = 4
ROLE = (2, 1, 3, 0)
TOK = 128
HALF, PART = TOK // 2, TOK // 4
SHARE = 192
WIDE = 768
PAD = 256
MESH = pl.DeviceIdType.MESH
F32, BF16 = jnp.float32, jnp.bfloat16


def remote(src, dst, send, recv, **where):
    return pltpu.make_async_remote_copy(
        src_ref=src, dst_ref=dst, send_sem=send, recv_sem=recv, device_id=where, device_id_type=MESH
    )


def kernel(
    ny, nz, nc,
    length_in, hidden, w_up, w_down, gain_in, leaf_in, parent_in,
    embed_out, centers_out, sums_out,
    len_ref, gain_ref, leaf_ref, parent_ref, xg, xt, upv, downv, pb, rsl, near, table, tables, pick_leaf, pick_parent, blocks, lab, wide,
    zbuf, zrecv, sbuf, srecv, qrecv, pbuf, precv,
    near_y, far_y, other_c, hops_z,
    local_sem, ag_send, ag_recv, f_send, f_recv, rs_send, rs_recv, d2_send, d2_recv,
    t_send, t_recv, s1_send, s1_recv, e_send, e_recv, z1_send, z1_recv,
    s2_send, s2_recv, q_send, q_recv, z2_send, z2_recv,
):
    y, z, c, x = (lax.axis_index(a) for a in (AY, AZ, AC, AX))
    plane = ny * nc
    here = y * nc + c
    right = {AX: lax.rem(x + 1, NX)}
    mates = [
        (lax.rem(y + dy, ny), lax.rem(c + dc, nc))
        for dy in sorted(range(ny), key=lambda d: -min(d, ny - d))
        for dc in reversed(range(nc))
    ]
    z_order = sorted(range(1, nz), key=lambda k: -min(k, nz - k))
    x_order = (2, 1, 3, 0)
    drain = []

    def signal(sem, **where):
        pl.semaphore_signal(sem, 1, device_id=where, device_id_type=MESH)

    def around(axis, at, size, step, sem):
        signal(sem, **{axis: lax.rem(at + step, size)})
        signal(sem, **{axis: lax.rem(at + size - step, size)})

    barrier = pltpu.get_barrier_semaphore()
    for k in (2, 1, 3):
        signal(barrier, **{AX: lax.rem(x + k, NX)})
    around(AY, y, ny, 1, barrier)
    around(AZ, z, nz, 1, barrier)
    signal(barrier, **{AC: 1 - c})
    loads = []
    def piece_of(device, p):
        first = pl.multiple_of(lax.rem(device + ROLE[p], NX) * TOK, TOK)
        return hidden.at[:, pl.ds(first, TOK)]

    for p in range(PIECES):
        loads.append(pltpu.make_async_copy(piece_of(x, p), xg.at[p, x], local_sem.at[p]))
    loads.append(pltpu.make_async_copy(w_up, upv, local_sem.at[PIECES]))
    loads.append(pltpu.make_async_copy(w_down, downv, local_sem.at[PIECES + 1]))
    small = [
        pltpu.make_async_copy(a, b, local_sem.at[PIECES + 2 + i])
        for i, (a, b) in enumerate(
            ((leaf_in, leaf_ref), (parent_in, parent_ref), (gain_in, gain_ref), (length_in, len_ref))
        )
    ]
    for load in small + loads:
        load.start()
    pl.semaphore_wait(barrier, 8)

    ag = {}

    def gather(p):
        for k in (1, 3, 2) if p == 0 else (1, 3):
            to = lax.rem(x + k, NX)
            copy = remote(piece_of(to, p), xg.at[p, x], ag_send.at[p, k], ag_recv.at[p, k], **{AX: to})
            copy.start()
            ag[p, k] = copy
            drain.append(copy.wait_send)

    for p in range(PIECES - 1):
        gather(p)
    passed = []

    def pass_on(n, p, k, step, rows):
        ag[p, k].wait_recv()
        source, to = lax.rem(x + NX - k, NX), {AX: lax.rem(x + k, NX)}
        passed.append(
            remote(xg.at[p, source, rows], xg.at[step, source, rows], f_send.at[n], f_recv.at[n], **to)
        )
        passed[n].start()
        drain.append(passed[n].wait_send)

    def collect(p):
        every, half = pl.ds(0, SHARE), SHARE // 2
        if p == 0:
            pass_on(0, 0, 1, 1, every)
            pass_on(1, 0, 3, 2, every)
            ag[0, 2].wait_recv()
        elif p == 1:
            pass_on(2, 1, 1, 3, pl.ds(0, half))
            ag[1, 3].wait_recv()
            passed[0].wait_recv()
        elif p == 2:
            pass_on(3, 2, 3, 3, pl.ds(half, half))
            ag[2, 1].wait_recv()
            passed[1].wait_recv()
        else:
            for copy in (ag[3, 1], ag[3, 3], passed[2], passed[3]):
                copy.wait_recv()

    around(AY, y, ny, 1, near_y)
    steps = [s for s in (1, 2, 4) if 2 * s <= nz // 2]
    if steps:
        around(AZ, z, nz, steps[0], hops_z.at[0])

    def handshake_2():
        pl.semaphore_wait(near_y, 2)
        around(AY, y, ny, 1, far_y)
        if len(steps) > 0:
            pl.semaphore_wait(hops_z.at[0], 2)
        if len(steps) > 1:
            around(AZ, z, nz, steps[1], hops_z.at[1])

    def handshake_3():
        pl.semaphore_wait(far_y, 2)
        signal(other_c, **{AC: 1 - c})
        if len(steps) > 1:
            pl.semaphore_wait(hops_z.at[1], 2)
        if len(steps) > 2:
            around(AZ, z, nz, steps[2], hops_z.at[2])

    def handshake_4():
        pl.semaphore_wait(other_c, 1)
        if len(steps) > 2:
            pl.semaphore_wait(hops_z.at[2], 2)

    for load in small:
        load.wait()
    table[...] = jnp.zeros_like(table)
    table[0:1, 0:LAB] = leaf_ref[...]
    table[1:2, 0:LEAF] = parent_ref[...]

    def compute(p):
        collect(p)
        features = xg[p].reshape(WIDE, TOK).T
        if p == PIECES - 1:
            xt[...] = features
        upward = jnp.dot(features, upv[...], preferred_element_type=F32)
        activ = (0.5 * upward * (1.0 + lax.erf(upward * (0.5**0.5)))).astype(BF16)
        pb[p] = jnp.dot(activ, downv[...], preferred_element_type=F32).astype(BF16)

    sides = ((0, 1, 0), (1, 3, HALF))
    joins, arrivals = {}, []

    def send(src, dst, send_sem, recv_sem, k):
        copy = remote(src, dst, send_sem, recv_sem, **{AX: lax.rem(x + k, NX)})
        copy.start()
        drain.append(copy.wait_send)
        return copy

    def finish(part):
        for side, k, first in sides:
            rows = pl.ds(first + PART * part, PART)
            joins[side, part].wait_recv()
            both = pb[1 + side, rows, :].astype(F32) + near[side, part].astype(F32)
            pb[1 + side, rows, :] = both.astype(BF16)
            arrivals.append(
                send(pb.at[1 + side, rows], rsl.at[side, rows], rs_send.at[side, part], rs_recv.at[side, part], k)
            )

    for load in loads:
        load.wait()
    compute(0)
    for part in range(2):
        for side, k, first in sides:
            rows = pl.ds(first + PART * part, PART)
            joins[side, part] = send(
                pb.at[0, rows], near.at[side, part], d2_send.at[side, part], d2_recv.at[side, part], k
            )
    gather(PIECES - 1)
    handshake_2()
    for side, k, first in sides:
        compute(1 + side)
        rows = pl.ds(HALF - first, HALF)
        arrivals.append(
            send(pb.at[1 + side, rows], rsl.at[side, rows], rs_send.at[side, 2], rs_recv.at[side, 2], k)
        )
    handshake_3()
    finish(0)
    finish(1)
    compute(PIECES - 1)
    handshake_4()

    for yy, cc in mates[:-1]:
        remote(table, tables.at[here], t_send, t_recv, **{AY: yy, AC: cc}).start()
    tables[here] = table[...]

    gain = gain_ref[...].reshape(1, WIDE)
    position = lax.broadcasted_iota(jnp.int32, (SEQ, 1), 0)
    embeds = {}

    def pool(label):
        rows = pl.ds(SEQ * label, SEQ)
        summed = pb[PIECES - 1, rows, :].astype(F32)
        for side in range(2):
            summed = summed + rsl[side, rows, :].astype(F32)
        mixed = (xt[rows, :].astype(F32) + summed).astype(BF16).astype(F32)
        mean = jnp.mean(mixed, axis=1, keepdims=True)
        centred = mixed - mean
        variance = jnp.mean(centred * centred, axis=1, keepdims=True)
        normed = centred * lax.rsqrt(variance + 1e-05) * gain
        length = len_ref[8 * x + label]
        kept = jnp.where(position < length, normed, 0.0)
        pooled = jnp.sum(kept, axis=0, keepdims=True) / length.astype(F32)
        embeds[label] = pooled * lax.rsqrt(jnp.mean(pooled * pooled, axis=1, keepdims=True) + 1e-05)

    for copies, group in ((arrivals[:4], (0, 1, 4, 5)), (arrivals[4:], (2, 3, 6, 7))):
        for copy in copies:
            copy.wait_recv()
        for label in group:
            pool(label)
    embed = jnp.concatenate([embeds[label] for label in range(8)], axis=0)
    zero = jnp.zeros((8, PAD - SHARE), F32)
    for s in range(NX):
        part = embed[:, SHARE * s : SHARE * (s + 1)]
        blocks[s] = jnp.concatenate([part, zero], axis=1).astype(BF16)

    slot = here * NX + x
    for n, (yy, cc) in enumerate(mates):
        for k in x_order:
            if k == 0 and n == plane - 1:
                continue
            to = lax.rem(x + k, NX)
            remote(blocks.at[to], lab.at[slot], s1_send, s1_recv, **{AY: yy, AC: cc, AX: to}).start()
    lab[slot] = blocks[x]
    wide[x] = blocks[...]

    others = tables.at[pl.ds(0, plane - 1)]
    others = remote(others, others, t_send, t_recv, **right)
    others.wait_recv()
    drain.append(others.wait_send)
    column = nz * LEAF
    row = lax.broadcasted_iota(jnp.int32, (column, 1), 0)
    leaf_of_row = ((y * nz + lax.div(row, LEAF)) * nc + c) * LEAF + lax.rem(row, LEAF)
    row2 = lax.broadcasted_iota(jnp.int32, (nz * PAR, 1), 0)
    parent_of_row = ((y * nz + lax.div(row2, PAR)) * nc + c) * PAR + lax.rem(row2, PAR)
    for k in range(plane):
        pick_leaf[:, LAB * k : LAB * (k + 1)] = (leaf_of_row == tables[k, 0:1, 0:LAB]).astype(F32)
        pick = (parent_of_row == tables[k, 1:2, 0:LEAF]).astype(F32)
        for part in range(3):
            first = (plane * part + k) * LEAF
            pick_parent[:, first : first + LEAF] = pick
    picked_leaf = pick_leaf[...].astype(BF16)

    got = lab.at[pl.ds(0, plane * NX - 1)]
    got = remote(got, got, s1_send, s1_recv, **right)
    drain.append(got.wait_send)
    got.wait_recv()
    labels = lab[...].astype(F32).reshape(plane * LAB, PAD).astype(BF16)
    leaf_part = jnp.dot(picked_leaf, labels, preferred_element_type=F32)
    zbuf[...] = leaf_part.reshape(nz, LEAF, PAD).astype(BF16)
    for k in z_order:
        to = lax.rem(z + k, nz)
        remote(zbuf.at[to], zrecv.at[z], z1_send, z1_recv, **{AZ: to}).start()
    zrecv[z] = zbuf[z]
    spread = []
    for k in (2, 1, 3):
        to = {AX: lax.rem(x + k, NX)}
        spread.append(remote(blocks, wide.at[x], e_send.at[k], e_recv.at[k], **to))
        spread[-1].start()
        drain.append(spread[-1].wait_send)

    for copy in spread:
        copy.wait_recv()
    whole = [
        jnp.concatenate([wide[s, b].astype(F32)[:, :SHARE] for b in range(NX)], axis=1) for s in range(NX)
    ]
    embed_out[...] = jnp.concatenate(whole, axis=0).astype(BF16)

    got = zrecv.at[pl.ds(0, nz - 1)]
    got = remote(got, got, z1_send, z1_recv, **right)
    drain.append(got.wait_send)
    got.wait_recv()
    leaf_sum = jnp.sum(zrecv[...].astype(F32), axis=0)
    square = jnp.sum(leaf_sum * leaf_sum, axis=1, keepdims=True)
    lane = lax.broadcasted_iota(jnp.int32, (LEAF, PAD), 1)
    sbuf[...] = jnp.where(lane < SHARE, leaf_sum, square)

    for n, (yy, cc) in enumerate(mates):
        for k in x_order:
            to = {AY: yy, AC: cc, AX: lax.rem(x + k, NX)}
            if k > 0:
                remote(sbuf.at[:, pl.ds(128, 128)], qrecv.at[x, here], q_send, q_recv, **to).start()
            elif n < plane - 1:
                remote(sbuf, srecv.at[here], s2_send, s2_recv, **to).start()
    srecv[here] = sbuf[...]
    qrecv[x] = jnp.zeros_like(qrecv[x])
    got = srecv.at[pl.ds(0, plane - 1)]
    got = remote(got, got, s2_send, s2_recv, **right)
    drain.append(got.wait_send)
    got.wait_recv()
    got = qrecv.at[pl.ds(0, NX - 1)]
    got = remote(got, got, q_send, q_recv, **right)
    drain.append(got.wait_send)
    got.wait_recv()
    sums = srecv[...]
    total = sums[:, :, PAD - 1 :] + jnp.sum(qrecv[...], axis=0)[:, :, 127:]
    centers = (sums * lax.rsqrt(total / WIDE + 1e-05)).reshape(plane * LEAF, PAD)
    parts = []
    rest = centers
    for part in range(3):
        parts.append(rest.astype(BF16))
        rest = rest - parts[-1].astype(F32)
    parent_part = jnp.dot(
        pick_parent[...].astype(BF16), jnp.concatenate(parts, axis=0), preferred_element_type=F32
    )
    for k in range(nz):
        pbuf[k] = parent_part[PAR * k : PAR * (k + 1)]
    for k in z_order:
        to = lax.rem(z + k, nz)
        remote(pbuf.at[to], precv.at[z], z2_send, z2_recv, **{AZ: to}).start()
    precv[z] = pbuf[z]
    mine = srecv[here]
    total = mine[:, PAD - 1 :]
    for s in range(NX):
        total = total + qrecv[s, here][:, 127:]
    centers_out[...] = (mine * lax.rsqrt(total / WIDE + 1e-05))[:, :SHARE]
    got = precv.at[pl.ds(0, nz - 1)]
    got = remote(got, got, z2_send, z2_recv, **right)
    drain.append(got.wait_send)
    got.wait_recv()
    sums_out[...] = jnp.sum(precv[...], axis=0)[:, :SHARE]
    for wait in drain:
        wait()


def hand_over(*refs):
    ins, outs = refs[:3], refs[3:6]
    for a, b in zip(ins, outs):
        b[...] = a[...]


def local(hidden_in, w_up, w_down, norm_gain, title_length, label_leaf, leaf_parent):
    ny, nz, nc = (lax.axis_size(a) for a in LABELS)
    plane = ny * nc
    vmem, dma, regular = pltpu.VMEM, pltpu.SemaphoreType.DMA, pltpu.SemaphoreType.REGULAR
    in_vmem = pl.BlockSpec(memory_space=pltpu.VMEM)
    anywhere = pl.BlockSpec(memory_space=pl.ANY)
    out_shape = (
        jax.ShapeDtypeStruct((LAB, WIDE), BF16),
        jax.ShapeDtypeStruct((LEAF, SHARE), F32),
        jax.ShapeDtypeStruct((PAR, SHARE), F32),
    )
    outs = pl.pallas_call(
        functools.partial(kernel, ny, nz, nc),
        out_shape=tuple(vmem(o.shape, o.dtype) for o in out_shape),
        in_specs=[anywhere] * 7,
        out_specs=(in_vmem,) * 3,
        scratch_shapes=[
            pltpu.SMEM((LAB,), jnp.int32),
            vmem((WIDE,), F32),
            vmem((1, LAB), jnp.int32),
            vmem((1, LEAF), jnp.int32),
            vmem((PIECES, NX, SHARE, TOK), BF16),
            vmem((TOK, WIDE), BF16),
            vmem((WIDE, WIDE), BF16),
            vmem((WIDE, WIDE), BF16),
            vmem((PIECES, TOK, WIDE), BF16),
            vmem((2, TOK, WIDE), BF16),
            vmem((2, 2, PART, WIDE), BF16),
            vmem((8, 128), jnp.int32),
            vmem((plane, 8, 128), jnp.int32),
            vmem((nz * LEAF, plane * LAB), F32),
            vmem((nz * PAR, 3 * plane * LEAF), F32),
            vmem((NX, 8, PAD), BF16),
            vmem((plane * NX, 8, PAD), BF16),
            vmem((NX, NX, 8, PAD), BF16),
            vmem((nz, LEAF, PAD), BF16),
            vmem((nz, LEAF, PAD), BF16),
            vmem((LEAF, PAD), F32),
            vmem((plane, LEAF, PAD), F32),
            vmem((NX, plane, LEAF, 128), F32),
            vmem((nz, PAR, PAD), F32),
            vmem((nz, PAR, PAD), F32),
            regular, regular, regular, regular((3,)),
            dma((PIECES + 6,)),
            dma((PIECES, NX)), dma((PIECES, NX)), dma((4,)), dma((4,)), dma((2, 3)), dma((2, 3)), dma((2, 2)), dma((2, 2)),
            dma(()), dma(()), dma(()), dma(()),
            dma((NX,)), dma((NX,)),
            dma(()), dma(()), dma(()), dma(()), dma(()), dma(()), dma(()), dma(()),
        ],
        compiler_params=pltpu.CompilerParams(collective_id=0, has_side_effects=True),
    )(
        title_length,
        hidden_in.T,
        w_up,
        w_down,
        norm_gain,
        label_leaf[None, :],
        leaf_parent[None, :],
    )
    return pl.pallas_call(
        hand_over,
        out_shape=out_shape,
        in_specs=[in_vmem] * 3,
        out_specs=(in_vmem,) * 3,
    )(*(pltpu.with_memory_space_constraint(o, pltpu.VMEM) for o in outs))


def solution(mesh):
    labels = mesh.shape["labels"]
    side = 4 if labels == 128 else 2
    split = Mesh(
        mesh.devices.reshape(side, labels // side // 2, 2, mesh.shape["heads"]), (AY, AZ, AC, AX)
    )
    placed = (P(LABELS, AX), P(None, AX), P(AX, None), P(), P(LABELS), P(LABELS), P(LABELS))
    return jax.shard_map(
        local,
        mesh=split,
        in_specs=placed,
        out_specs=(P(LABELS, None), P(LABELS, AX), P(LABELS, AX)),
        check_vma=False,
    )
```

```python
import functools

import jax
import jax.numpy as jnp
from jax import lax
from jax.experimental import pallas as pl
from jax.experimental.pallas import tpu as pltpu
from jax.sharding import Mesh
from jax.sharding import PartitionSpec as P

AY, AZ, AC, AX = "labels_0", "labels_1", "labels_2", "heads"
LABELS = (AY, AZ, AC)
NX = 4
SEQ = 16
LAB = 32
LEAF = 8
PAR = 2
PIECES = 4
ROLE = (2, 1, 3, 0)
TOK = 128
HALF, PART = TOK // 2, TOK // 4
SHARE = 192
WIDE = 768
PAD = 256
MESH = pl.DeviceIdType.MESH
F32, BF16 = jnp.float32, jnp.bfloat16


def remote(src, dst, send, recv, **where):
    return pltpu.make_async_remote_copy(
        src_ref=src, dst_ref=dst, send_sem=send, recv_sem=recv, device_id=where, device_id_type=MESH
    )


def kernel(
    ny, nz, nc,
    length_in, hidden, w_up, w_down, gain_in, leaf_in, parent_in,
    embed_out, centers_out, sums_out,
    len_ref, gain_ref, leaf_ref, parent_ref, xg, xt, upv, downv, pb, rsl, near, table, tables, pick_leaf, pick_parent, blocks, lab, wide,
    zbuf, zrecv, sbuf, srecv, sqrow, qrecv, pbuf, precv,
    near_y, far_y, other_c, hops_z,
    local_sem, ag_send, ag_recv, f_send, f_recv, rs_send, rs_recv, d2_send, d2_recv,
    t_send, t_recv, s1_send, s1_recv, e_send, e_recv, z1_send, z1_recv,
    s2_send, s2_recv, q_send, q_recv, z2_send, z2_recv,
):
    y, z, c, x = (lax.axis_index(a) for a in (AY, AZ, AC, AX))
    plane = ny * nc
    here = y * nc + c
    right = {AX: lax.rem(x + 1, NX)}
    mates = [
        (lax.rem(y + dy, ny), lax.rem(c + dc, nc))
        for dy in sorted(range(ny), key=lambda d: -min(d, ny - d))
        for dc in reversed(range(nc))
    ]
    z_order = sorted(range(1, nz), key=lambda k: -min(k, nz - k))
    x_order = (2, 1, 3, 0)
    drain = []

    def signal(sem, **where):
        pl.semaphore_signal(sem, 1, device_id=where, device_id_type=MESH)

    def around(axis, at, size, step, sem):
        signal(sem, **{axis: lax.rem(at + step, size)})
        signal(sem, **{axis: lax.rem(at + size - step, size)})

    barrier = pltpu.get_barrier_semaphore()
    for k in (2, 1, 3):
        signal(barrier, **{AX: lax.rem(x + k, NX)})
    around(AY, y, ny, 1, barrier)
    around(AZ, z, nz, 1, barrier)
    signal(barrier, **{AC: 1 - c})
    loads = []
    def piece_of(device, p):
        first = pl.multiple_of(lax.rem(device + ROLE[p], NX) * TOK, TOK)
        return hidden.at[:, pl.ds(first, TOK)]

    for p in range(PIECES):
        loads.append(pltpu.make_async_copy(piece_of(x, p), xg.at[p, x], local_sem.at[p]))
    loads.append(pltpu.make_async_copy(w_up, upv, local_sem.at[PIECES]))
    loads.append(pltpu.make_async_copy(w_down, downv, local_sem.at[PIECES + 1]))
    small = [
        pltpu.make_async_copy(a, b, local_sem.at[PIECES + 2 + i])
        for i, (a, b) in enumerate(
            ((leaf_in, leaf_ref), (parent_in, parent_ref), (gain_in, gain_ref), (length_in, len_ref))
        )
    ]
    for load in small + loads:
        load.start()
    pl.semaphore_wait(barrier, 8)

    ag = {}

    def gather(p):
        for k in (1, 3, 2) if p == 0 else (1, 3):
            to = lax.rem(x + k, NX)
            copy = remote(piece_of(to, p), xg.at[p, x], ag_send.at[p, k], ag_recv.at[p, k], **{AX: to})
            copy.start()
            ag[p, k] = copy
            drain.append(copy.wait_send)

    for p in range(PIECES - 1):
        gather(p)
    passed = []

    def pass_on(n, p, k, step, rows):
        ag[p, k].wait_recv()
        source, to = lax.rem(x + NX - k, NX), {AX: lax.rem(x + k, NX)}
        passed.append(
            remote(xg.at[p, source, rows], xg.at[step, source, rows], f_send.at[n], f_recv.at[n], **to)
        )
        passed[n].start()
        drain.append(passed[n].wait_send)

    def collect(p):
        every, half = pl.ds(0, SHARE), SHARE // 2
        if p == 0:
            pass_on(0, 0, 1, 1, every)
            pass_on(1, 0, 3, 2, every)
            gather(PIECES - 1)
            ag[0, 2].wait_recv()
        elif p == 1:
            pass_on(2, 1, 1, 3, pl.ds(0, half))
            ag[1, 3].wait_recv()
            passed[0].wait_recv()
        elif p == 2:
            pass_on(3, 2, 3, 3, pl.ds(half, half))
            ag[2, 1].wait_recv()
            passed[1].wait_recv()
        else:
            for copy in (ag[3, 1], ag[3, 3], passed[2], passed[3]):
                copy.wait_recv()

    around(AY, y, ny, 1, near_y)
    steps = [s for s in (1, 2, 4) if 2 * s <= nz // 2]
    if steps:
        around(AZ, z, nz, steps[0], hops_z.at[0])

    def handshake_2():
        pl.semaphore_wait(near_y, 2)
        around(AY, y, ny, 1, far_y)
        if len(steps) > 0:
            pl.semaphore_wait(hops_z.at[0], 2)
        if len(steps) > 1:
            around(AZ, z, nz, steps[1], hops_z.at[1])

    def handshake_3():
        pl.semaphore_wait(far_y, 2)
        signal(other_c, **{AC: 1 - c})
        if len(steps) > 1:
            pl.semaphore_wait(hops_z.at[1], 2)
        if len(steps) > 2:
            around(AZ, z, nz, steps[2], hops_z.at[2])

    def handshake_4():
        pl.semaphore_wait(other_c, 1)
        if len(steps) > 2:
            pl.semaphore_wait(hops_z.at[2], 2)

    for load in small:
        load.wait()
    table[...] = jnp.zeros_like(table)
    table[0:1, 0:LAB] = leaf_ref[...]
    table[1:2, 0:LEAF] = parent_ref[...]

    def compute(p):
        collect(p)
        features = xg[p].reshape(WIDE, TOK).T
        if p == PIECES - 1:
            xt[...] = features
        upward = jnp.dot(features, upv[...], preferred_element_type=F32)
        activ = (0.5 * upward * (1.0 + lax.erf(upward * (0.5**0.5)))).astype(BF16)
        pb[p] = jnp.dot(activ, downv[...], preferred_element_type=F32).astype(BF16)

    sides = ((0, 1, 0), (1, 3, HALF))
    joins, arrivals = {}, []

    def send(src, dst, send_sem, recv_sem, k):
        copy = remote(src, dst, send_sem, recv_sem, **{AX: lax.rem(x + k, NX)})
        copy.start()
        drain.append(copy.wait_send)
        return copy

    def finish(part):
        for side, k, first in sides:
            rows = pl.ds(first + PART * part, PART)
            joins[side, part].wait_recv()
            both = pb[1 + side, rows, :].astype(F32) + near[side, part].astype(F32)
            pb[1 + side, rows, :] = both.astype(BF16)
            arrivals.append(
                send(pb.at[1 + side, rows], rsl.at[side, rows], rs_send.at[side, part], rs_recv.at[side, part], k)
            )

    for load in loads:
        load.wait()
    compute(0)
    for part in range(2):
        for side, k, first in sides:
            rows = pl.ds(first + PART * part, PART)
            joins[side, part] = send(
                pb.at[0, rows], near.at[side, part], d2_send.at[side, part], d2_recv.at[side, part], k
            )
    handshake_2()
    for side, k, first in sides:
        compute(1 + side)
        rows = pl.ds(HALF - first, HALF)
        arrivals.append(
            send(pb.at[1 + side, rows], rsl.at[side, rows], rs_send.at[side, 2], rs_recv.at[side, 2], k)
        )
    handshake_3()
    finish(0)
    finish(1)
    compute(PIECES - 1)
    handshake_4()

    for yy, cc in mates[:-1]:
        remote(table, tables.at[here], t_send, t_recv, **{AY: yy, AC: cc}).start()
    tables[here] = table[...]

    gain = gain_ref[...].reshape(1, WIDE)
    position = lax.broadcasted_iota(jnp.int32, (SEQ, 1), 0)
    embeds = {}

    def pool(label):
        rows = pl.ds(SEQ * label, SEQ)
        summed = pb[PIECES - 1, rows, :].astype(F32)
        for side in range(2):
            summed = summed + rsl[side, rows, :].astype(F32)
        mixed = (xt[rows, :].astype(F32) + summed).astype(BF16).astype(F32)
        mean = jnp.mean(mixed, axis=1, keepdims=True)
        centred = mixed - mean
        variance = jnp.mean(centred * centred, axis=1, keepdims=True)
        normed = centred * lax.rsqrt(variance + 1e-05) * gain
        length = len_ref[8 * x + label]
        kept = jnp.where(position < length, normed, 0.0)
        pooled = jnp.sum(kept, axis=0, keepdims=True) / length.astype(F32)
        embeds[label] = pooled * lax.rsqrt(jnp.mean(pooled * pooled, axis=1, keepdims=True) + 1e-05)

    for copies, group in ((arrivals[:4], (0, 1, 4, 5)), (arrivals[4:], (2, 3, 6, 7))):
        for copy in copies:
            copy.wait_recv()
        for label in group:
            pool(label)
    embed = jnp.concatenate([embeds[label] for label in range(8)], axis=0)
    zero = jnp.zeros((8, PAD - SHARE), F32)
    for s in range(NX):
        part = embed[:, SHARE * s : SHARE * (s + 1)]
        blocks[s] = jnp.concatenate([part, zero], axis=1).astype(BF16)

    slot = here * NX + x
    for n, (yy, cc) in enumerate(mates):
        for k in x_order:
            if k == 0 and n == plane - 1:
                continue
            to = lax.rem(x + k, NX)
            remote(blocks.at[to], lab.at[slot], s1_send, s1_recv, **{AY: yy, AC: cc, AX: to}).start()
    lab[slot] = blocks[x]
    wide[x] = blocks[...]

    others = tables.at[pl.ds(0, plane - 1)]
    others = remote(others, others, t_send, t_recv, **right)
    others.wait_recv()
    drain.append(others.wait_send)
    column = nz * LEAF
    row = lax.broadcasted_iota(jnp.int32, (column, 1), 0)
    leaf_of_row = ((y * nz + lax.div(row, LEAF)) * nc + c) * LEAF + lax.rem(row, LEAF)
    row2 = lax.broadcasted_iota(jnp.int32, (nz * PAR, 1), 0)
    parent_of_row = ((y * nz + lax.div(row2, PAR)) * nc + c) * PAR + lax.rem(row2, PAR)
    for k in range(plane):
        pick_leaf[:, LAB * k : LAB * (k + 1)] = (leaf_of_row == tables[k, 0:1, 0:LAB]).astype(F32)
        pick = (parent_of_row == tables[k, 1:2, 0:LEAF]).astype(F32)
        for part in range(3):
            first = (plane * part + k) * LEAF
            pick_parent[:, first : first + LEAF] = pick
    picked_leaf = pick_leaf[...].astype(BF16)

    got = lab.at[pl.ds(0, plane * NX - 1)]
    got = remote(got, got, s1_send, s1_recv, **right)
    drain.append(got.wait_send)
    got.wait_recv()
    labels = lab[...].astype(F32).reshape(plane * LAB, PAD).astype(BF16)
    leaf_part = jnp.dot(picked_leaf, labels, preferred_element_type=F32)
    zbuf[...] = leaf_part.reshape(nz, LEAF, PAD).astype(BF16)
    for k in z_order:
        to = lax.rem(z + k, nz)
        remote(zbuf.at[to], zrecv.at[z], z1_send, z1_recv, **{AZ: to}).start()
    zrecv[z] = zbuf[z]
    spread = []
    for k in (2, 1, 3):
        to = {AX: lax.rem(x + k, NX)}
        spread.append(remote(blocks, wide.at[x], e_send.at[k], e_recv.at[k], **to))
        spread[-1].start()
        drain.append(spread[-1].wait_send)

    for copy in spread:
        copy.wait_recv()
    whole = [
        jnp.concatenate([wide[s, b].astype(F32)[:, :SHARE] for b in range(NX)], axis=1) for s in range(NX)
    ]
    embed_out[...] = jnp.concatenate(whole, axis=0).astype(BF16)

    got = zrecv.at[pl.ds(0, nz - 1)]
    got = remote(got, got, z1_send, z1_recv, **right)
    drain.append(got.wait_send)
    got.wait_recv()
    leaf_sum = jnp.sum(zrecv[...].astype(F32), axis=0)
    square = jnp.sum(leaf_sum * leaf_sum, axis=1, keepdims=True)
    sbuf[...] = leaf_sum
    diagonal = lax.broadcasted_iota(jnp.int32, (LEAF, 128), 0) == lax.broadcasted_iota(jnp.int32, (LEAF, 128), 1)
    sqrow[...] = jnp.sum(jnp.where(diagonal, square, 0.0), axis=0, keepdims=True)

    for n, (yy, cc) in enumerate(mates):
        for k in x_order:
            to = {AY: yy, AC: cc, AX: lax.rem(x + k, NX)}
            if k > 0 or n < plane - 1:
                remote(sqrow, qrecv.at[x * plane + here], q_send, q_recv, **to).start()
            if k == 0 and n < plane - 1:
                remote(sbuf, srecv.at[here], s2_send, s2_recv, **to).start()
    qrecv[x * plane + here] = sqrow[...]
    srecv[here] = sbuf[...]
    got = srecv.at[pl.ds(0, plane - 1)]
    got = remote(got, got, s2_send, s2_recv, **right)
    drain.append(got.wait_send)
    got.wait_recv()
    got = qrecv.at[pl.ds(0, NX * plane - 1)]
    got = remote(got, got, q_send, q_recv, **right)
    drain.append(got.wait_send)
    got.wait_recv()
    sums = srecv[...]
    rows = jnp.sum(qrecv[...].reshape(NX, plane, 1, 128), axis=0)
    total = jnp.sum(jnp.where(diagonal[None], rows, 0.0), axis=2, keepdims=True)
    centers = (sums * lax.rsqrt(total / WIDE + 1e-05)).reshape(plane * LEAF, PAD)
    parts = []
    rest = centers
    for part in range(3):
        parts.append(rest.astype(BF16))
        rest = rest - parts[-1].astype(F32)
    parent_part = jnp.dot(
        pick_parent[...].astype(BF16), jnp.concatenate(parts, axis=0), preferred_element_type=F32
    )
    for k in range(nz):
        pbuf[k] = parent_part[PAR * k : PAR * (k + 1)]
    for k in z_order:
        to = lax.rem(z + k, nz)
        remote(pbuf.at[to], precv.at[z], z2_send, z2_recv, **{AZ: to}).start()
    precv[z] = pbuf[z]
    mine = srecv[here]
    row = qrecv[here]
    for s in range(1, NX):
        row = row + qrecv[s * plane + here]
    total = jnp.sum(jnp.where(diagonal, row, 0.0), axis=1, keepdims=True)
    centers_out[...] = (mine * lax.rsqrt(total / WIDE + 1e-05))[:, :SHARE]
    got = precv.at[pl.ds(0, nz - 1)]
    got = remote(got, got, z2_send, z2_recv, **right)
    drain.append(got.wait_send)
    got.wait_recv()
    sums_out[...] = jnp.sum(precv[...], axis=0)[:, :SHARE]
    for wait in drain:
        wait()


def hand_over(*refs):
    ins, outs = refs[:3], refs[3:6]
    for a, b in zip(ins, outs):
        b[...] = a[...]


def local(hidden_in, w_up, w_down, norm_gain, title_length, label_leaf, leaf_parent):
    ny, nz, nc = (lax.axis_size(a) for a in LABELS)
    plane = ny * nc
    vmem, dma, regular = pltpu.VMEM, pltpu.SemaphoreType.DMA, pltpu.SemaphoreType.REGULAR
    in_vmem = pl.BlockSpec(memory_space=pltpu.VMEM)
    anywhere = pl.BlockSpec(memory_space=pl.ANY)
    out_shape = (
        jax.ShapeDtypeStruct((LAB, WIDE), BF16),
        jax.ShapeDtypeStruct((LEAF, SHARE), F32),
        jax.ShapeDtypeStruct((PAR, SHARE), F32),
    )
    outs = pl.pallas_call(
        functools.partial(kernel, ny, nz, nc),
        out_shape=tuple(vmem(o.shape, o.dtype) for o in out_shape),
        in_specs=[anywhere] * 7,
        out_specs=(in_vmem,) * 3,
        scratch_shapes=[
            pltpu.SMEM((LAB,), jnp.int32),
            vmem((WIDE,), F32),
            vmem((1, LAB), jnp.int32),
            vmem((1, LEAF), jnp.int32),
            vmem((PIECES, NX, SHARE, TOK), BF16),
            vmem((TOK, WIDE), BF16),
            vmem((WIDE, WIDE), BF16),
            vmem((WIDE, WIDE), BF16),
            vmem((PIECES, TOK, WIDE), BF16),
            vmem((2, TOK, WIDE), BF16),
            vmem((2, 2, PART, WIDE), BF16),
            vmem((8, 128), jnp.int32),
            vmem((plane, 8, 128), jnp.int32),
            vmem((nz * LEAF, plane * LAB), F32),
            vmem((nz * PAR, 3 * plane * LEAF), F32),
            vmem((NX, 8, PAD), BF16),
            vmem((plane * NX, 8, PAD), BF16),
            vmem((NX, NX, 8, PAD), BF16),
            vmem((nz, LEAF, PAD), BF16),
            vmem((nz, LEAF, PAD), BF16),
            vmem((LEAF, PAD), F32),
            vmem((plane, LEAF, PAD), F32),
            vmem((1, 128), F32),
            vmem((NX * plane, 1, 128), F32),
            vmem((nz, PAR, PAD), F32),
            vmem((nz, PAR, PAD), F32),
            regular, regular, regular, regular((3,)),
            dma((PIECES + 6,)),
            dma((PIECES, NX)), dma((PIECES, NX)), dma((4,)), dma((4,)), dma((2, 3)), dma((2, 3)), dma((2, 2)), dma((2, 2)),
            dma(()), dma(()), dma(()), dma(()),
            dma((NX,)), dma((NX,)),
            dma(()), dma(()), dma(()), dma(()), dma(()), dma(()), dma(()), dma(()),
        ],
        compiler_params=pltpu.CompilerParams(collective_id=0, has_side_effects=True),
    )(
        title_length,
        hidden_in.T,
        w_up,
        w_down,
        norm_gain,
        label_leaf[None, :],
        leaf_parent[None, :],
    )
    return pl.pallas_call(
        hand_over,
        out_shape=out_shape,
        in_specs=[in_vmem] * 3,
        out_specs=(in_vmem,) * 3,
    )(*(pltpu.with_memory_space_constraint(o, pltpu.VMEM) for o in outs))


def solution(mesh):
    labels = mesh.shape["labels"]
    side = 4 if labels == 128 else 2
    split = Mesh(
        mesh.devices.reshape(side, labels // side // 2, 2, mesh.shape["heads"]), (AY, AZ, AC, AX)
    )
    placed = (P(LABELS, AX), P(None, AX), P(AX, None), P(), P(LABELS), P(LABELS), P(LABELS))
    return jax.shard_map(
        local,
        mesh=split,
        in_specs=placed,
        out_specs=(P(LABELS, None), P(LABELS, AX), P(LABELS, AX)),
        check_vma=False,
    )
```
